256 devices in a mesh: dp: 32 (over x, y, core), mp: 8 (over z).
Axes of the slice: x: 4, y: 4, z: 8, core: 2. Of those that a mesh axis runs over, the one named last changes fastest.
Arguments:
- queries: bfloat16 [4096, 64, 128], P('dp', 'mp'), may hold values from -6 to 6
- key_cache: bfloat16 [4096, 8, 128, 128], P('dp', 'mp'), may hold values from -6 to 6
- value_cache: bfloat16 [4096, 8, 128, 128], P('dp', 'mp'), may hold values from -6 to 6
- key_new: bfloat16 [4096, 8, 128], P('dp', 'mp'), may hold values from -6 to 6
- value_new: bfloat16 [4096, 8, 128], P('dp', 'mp'), may hold values from -6 to 6
- lengths: int32 [4096], P('dp'), may hold values from 1 to 128, as said below
- occupied: int32 [4096], P('dp'), may hold values 0 or 1
- slot_request: int32 [4096], P('dp'), may hold values from 0 to 4095, as said below
- request_adapter: int32 [4096], replicated, may hold values from 0 to 63, as said below
- out_weight: bfloat16 [8192, 4096], P('mp'), may hold values from -0.375 to 0.375
- shrink_weight: bfloat16 [64, 8192, 64], P('dp', 'mp'), may hold values from -0.375 to 0.375
- expand_weight: bfloat16 [64, 64, 4096], P('dp', None, 'mp'), may hold values from -0.75 to 0.75
Outputs:
- mixed: bfloat16 [4096, 4096], P('dp', 'mp')
The draws below stay inside these ranges and needn't reach their ends.
Inputs may be any that keep to these rules, and one draw needn't show every extreme that they name: `slot_request`: A permutation: each request stands in exactly one slot. `request_adapter`: adapter n is owned by dp index n // 2. Among the slots of one dp index, at most 8 hold requests whose adapters one dp index owns; in every draw some dp index owns the adapters of exactly 8 slots of every dp index. `lengths`: each dp index has a slot of length 128.
All inputs are finite; a program needn't handle non-finite values. No bound on the sum of `occupied` on one device may be relied on, other than what follows from the above.
Results may differ from the reference program's by a relative error of at most 0.011.
Values may be sent and summed in bfloat16 or wider, within the bound.
A program may use at most 64 MiB of HBM per device.

```python
import math
import jax
import jax.numpy as jnp
from jax import lax

D = 8192
HQ = 64
KVH = 8
HD = 128
DOUT = 4096
R = 64
RQ_DEV = 128
CACHE = 128
ADP_DEV = 2
SLOTS = 4096
NADP = 64
CAP = 8


def routing(key):
    owners_count = SLOTS // RQ_DEV
    tickets = owners_count * CAP
    hot_owner = jax.random.randint(jax.random.fold_in(key, 101), (), 0, owners_count)
    ticket_owner = jnp.arange(tickets, dtype=jnp.int32) // CAP

    def block(number):
        block_key = jax.random.fold_in(jax.random.fold_in(key, 102), number)
        shuffled = jax.random.permutation(block_key, tickets).astype(jnp.int32)
        scores = jnp.where(ticket_owner == hot_owner, -1, shuffled)
        ranking = jnp.argsort(scores, stable=True)
        chosen = ticket_owner[ranking[:RQ_DEV]]
        mixing = jax.random.permutation(jax.random.fold_in(block_key, 1), RQ_DEV)
        local_ids = jax.random.randint(jax.random.fold_in(block_key, 2), (RQ_DEV,), 0, ADP_DEV)
        return chosen[mixing] * ADP_DEV + local_ids
    slot_adapter = jax.vmap(block)(jnp.arange(owners_count)).reshape(SLOTS).astype(jnp.int32)
    placement = jax.random.permutation(jax.random.fold_in(key, 103), SLOTS).astype(jnp.int32)
    by_request = jnp.zeros((SLOTS,), jnp.int32).at[placement].set(slot_adapter)
    return (placement, by_request)


def draw_slot_request(key, part):
    return routing(key)[0]


def draw_request_adapter(key, part):
    return routing(key)[1]


def draw_lengths(key, part):
    owners_count = SLOTS // RQ_DEV
    drawn = jax.random.randint(jax.random.fold_in(key, 201), (owners_count, RQ_DEV), 1, CACHE + 1)
    full_at = jax.random.randint(jax.random.fold_in(key, 202), (owners_count,), 0, RQ_DEV)
    drawn = drawn.at[jnp.arange(owners_count), full_at].set(CACHE)
    return drawn.reshape(SLOTS).astype(jnp.int32)


def attention_draws(key):
    queries = jnp.clip(jax.random.normal(jax.random.fold_in(key, 301), (SLOTS, HQ, HD), jnp.float32), -6.0, 6.0)
    cached = jnp.clip(jax.random.normal(jax.random.fold_in(key, 302), (SLOTS, KVH, CACHE, HD), jnp.float32), -6.0, 6.0)
    fresh = jnp.clip(jax.random.normal(jax.random.fold_in(key, 303), (SLOTS, KVH, HD), jnp.float32), -6.0, 6.0)
    return (queries, cached, fresh)


def draw_queries(key, part):
    return attention_draws(key)[0].astype(jnp.bfloat16)


def draw_key_cache(key, part):
    return attention_draws(key)[1].astype(jnp.bfloat16)


def draw_key_new(key, part):
    return attention_draws(key)[2].astype(jnp.bfloat16)


def set_ends(entries, own_key, least, high):
    longest = entries.shape.index(max(entries.shape))
    spots = []
    for shift in (0, 1):
        where = [jax.random.randint(jax.random.fold_in(own_key, axis), (), 0, length) for axis, length in enumerate(entries.shape)]
        where[longest] = (where[longest] + shift) % entries.shape[longest]
        spots.append(tuple(where))
    return entries.at[spots[0]].set(least).at[spots[1]].set(high)


def shard_levels(own_key, extent, cuts, least, top_value):
    gain, own = 1.0, jax.random.fold_in(own_key, 6)
    for dim, parts in cuts:
        draws = jnp.exp(jax.random.uniform(jax.random.fold_in(own, dim), (parts,), jnp.float32, least / len(cuts), top_value / len(cuts)))
        gain = gain * jnp.repeat(draws, extent[dim] // parts).reshape([-1 if axis == dim else 1 for axis in range(len(extent))])
    return gain


def centred(own_key, extent, scale, limit, cuts=(), kind=jnp.bfloat16):
    level = shard_levels(own_key, extent, cuts, -0.22, 0.18) if cuts else 1.0
    values = jax.random.normal(own_key, extent, jnp.float32) * scale * level
    return jnp.minimum(jnp.maximum(values, -limit), limit).astype(kind)


def setup_inputs(seed: int = 0) -> dict:
    streams_of = jax.random.split(jax.random.key(seed), 13)
    queries = draw_queries(jax.random.fold_in(streams_of[12], 71), 0)
    key_cache = draw_key_cache(jax.random.fold_in(streams_of[12], 71), 0)
    value_cache = centred(streams_of[2], (SLOTS, KVH, CACHE, HD), 1.0, 6.0, ((0, 32), (1, 8)))
    key_new = draw_key_new(jax.random.fold_in(streams_of[12], 71), 0)
    value_new = centred(streams_of[4], (SLOTS, KVH, HD), 1.0, 6.0, ((0, 32), (1, 8)))
    lengths = draw_lengths(jax.random.fold_in(streams_of[12], 71), 0)
    occupied = set_ends((jax.random.randint(streams_of[6], (SLOTS,), 0, 4) < 3).astype(jnp.int32), jax.random.fold_in(streams_of[6], 1), 0, 1)
    slot_request = draw_slot_request(jax.random.fold_in(streams_of[12], 71), 0)
    request_adapter = draw_request_adapter(jax.random.fold_in(streams_of[12], 71), 0)
    out_weight = centred(streams_of[9], (D, DOUT), (D // 32) ** -0.5, 0.375, ((0, 8),))
    shrink_weight = centred(streams_of[10], (NADP, D, R), (D // 32) ** -0.5, 0.375, ((0, 32), (1, 8)))
    expand_weight = centred(streams_of[11], (NADP, R, DOUT), R ** -0.5, 0.75, ((0, 32), (2, 8)))
    return dict(queries=queries, key_cache=key_cache, value_cache=value_cache, key_new=key_new, value_new=value_new, lengths=lengths, occupied=occupied, slot_request=slot_request, request_adapter=request_adapter, out_weight=out_weight, shrink_weight=shrink_weight, expand_weight=expand_weight)


def attend(queries, key_cache, value_cache, key_new, value_new, lengths):
    rows, heads, width = queries.shape
    kv_heads = key_cache.shape[1]
    group = heads // kv_heads
    inverse = 1.0 / math.sqrt(width)
    grouped = queries.astype(jnp.float32).reshape(rows, kv_heads, group, width)
    cached = jnp.einsum('bgjd,bgtd->bgjt', grouped, key_cache.astype(jnp.float32)) * inverse
    fresh = jnp.einsum('bgjd,bgd->bgj', grouped, key_new.astype(jnp.float32)) * inverse
    valid = jnp.arange(key_cache.shape[2])[None, :] < lengths[:, None]
    cached = jnp.where(valid[:, None, None, :], cached, -jnp.inf)
    top = jnp.maximum(lax.optimization_barrier(jnp.max(cached, axis=-1)), fresh)
    cached_exp = jnp.exp(cached - top[..., None])
    fresh_exp = jnp.exp(fresh - top)
    total = lax.optimization_barrier(jnp.sum(cached_exp, axis=-1)) + fresh_exp
    cached_w = (cached_exp / total[..., None]).astype(jnp.bfloat16)
    fresh_w = (fresh_exp / total).astype(jnp.bfloat16)
    summed = jnp.einsum('bgjt,bgtd->bgjd', cached_w.astype(jnp.float32), value_cache.astype(jnp.float32))
    summed = summed + fresh_w.astype(jnp.float32)[..., None] * value_new.astype(jnp.float32)[:, :, None, :]
    return summed.reshape(rows, heads * width).astype(jnp.bfloat16)

def reference(queries, key_cache, value_cache, key_new, value_new, lengths, occupied, slot_request, request_adapter, out_weight, shrink_weight, expand_weight):
    blocks = SLOTS // RQ_DEV

    def blocked(array):
        return array.reshape((blocks, RQ_DEV) + array.shape[1:])
    slot_adapter = request_adapter[slot_request]

    def one_block(pieces):
        q_rows, k_rows, v_rows, kn_rows, vn_rows, len_rows, adapter_rows = pieces
        attended = attend(q_rows, k_rows, v_rows, kn_rows, vn_rows, len_rows)
        base = jnp.dot(attended, out_weight, preferred_element_type=jnp.float32)
        shrink = shrink_weight[adapter_rows].astype(jnp.float32)
        low = jnp.einsum('bd,bdr->br', attended.astype(jnp.float32), shrink).astype(jnp.bfloat16)
        expand = expand_weight[adapter_rows].astype(jnp.float32)
        delta = (0.5 * jnp.einsum('br,bre->be', low.astype(jnp.float32), expand)).astype(jnp.bfloat16)
        return base + delta.astype(jnp.float32)
    mixed = lax.map(one_block, (blocked(queries), blocked(key_cache), blocked(value_cache), blocked(key_new), blocked(value_new), blocked(lengths), blocked(slot_adapter)))
    mixed = mixed.reshape(SLOTS, DOUT)
    return (occupied.astype(jnp.float32)[:, None] * mixed).astype(jnp.bfloat16)
```

```python
import functools
import math

import jax
import jax.numpy as jnp
from jax import lax
from jax.experimental import pallas as pl
from jax.experimental.pallas import tpu as pltpu
from jax.sharding import PartitionSpec as P

MESH = pl.DeviceIdType.MESH
BF = jnp.bfloat16
F32 = jnp.float32
CHUNK = 16


def nt_dot(a, b):
    return lax.dot_general(a, b, (((1,), (1,)), ((), ())), preferred_element_type=F32)


def nn_dot(a, b):
    return jnp.dot(a, b, preferred_element_type=F32)


def chain_messages(half):
    messages = [(half, 0)]
    for left in range(half - 1, 0, -1):
        messages += [(left, 1), (left, 0)]
    return messages


def kernel(
    n,
    mp,
    cap,
    lens_hbm,
    occ_hbm,
    sreq_hbm,
    radp_hbm,
    q_hbm,
    k_hbm,
    v_hbm,
    kn_hbm,
    vn_hbm,
    w_hbm,
    shr_hbm,
    exp_hbm,
    out_ref,
    lens,
    occ,
    sreq,
    radp,
    qbuf,
    kbuf,
    vbuf,
    knb,
    vnb,
    knf,
    vnf,
    wbuf,
    shr,
    expw,
    obuf,
    att,
    disp,
    comb,
    ids_out,
    ids_in,
    rows_out,
    rows_in,
    part,
    msg_out,
    msg_in,
    base,
    rs_out,
    rs_in,
    ag_out,
    ag_in,
    back_out,
    back_in,
    small_sem,
    k_sem,
    v_sem,
    w_sem,
    ids_sems,
    rows_sems,
    rs_sems,
    ag_sems,
    back_sems,
    msg_send,
    msg_recv,
):
    d = lax.axis_index("dp")
    m = lax.axis_index("mp")
    slots = lens.shape[1]
    heads = qbuf.shape[0] // slots
    width = qbuf.shape[1]
    outw = expw.shape[1]
    codes = n * cap
    group = codes // mp
    half_group = group // 2
    half = mp // 2
    inverse = 1.0 / math.sqrt(width)
    chunks = slots // CHUNK
    side = slots // 2

    smalls = [
        pltpu.make_async_copy(src, dst, small_sem.at[i])
        for i, (src, dst) in enumerate(
            [
                (lens_hbm, lens),
                (q_hbm, qbuf),
                (kn_hbm, knb),
                (vn_hbm, vnb),
                (sreq_hbm, sreq),
                (radp_hbm, radp),
                (occ_hbm, occ),
                (shr_hbm, shr),
                (exp_hbm, expw),
            ]
        )
    ]

    def k_copy(c):
        rows = pl.ds(c * CHUNK, CHUNK)
        return pltpu.make_async_copy(k_hbm.at[rows], kbuf.at[rows], k_sem.at[c])

    def v_copy(c):
        rows = pl.ds(c * CHUNK, CHUNK)
        return pltpu.make_async_copy(v_hbm.at[rows], vbuf.at[rows], v_sem.at[c])

    offsets = [half]
    for r in range(half - 1, 0, -1):
        offsets += [r, -r]
    offsets += [0]

    def w_copy(i):
        block = lax.rem(m + offsets[i] + mp, mp)
        cols = pl.ds(pl.multiple_of(block * outw, outw), outw)
        return pltpu.make_async_copy(w_hbm.at[:, cols], wbuf.at[i], w_sem.at[i])

    for copy in smalls[:4]:
        copy.start()
    k_copy(0).start()
    v_copy(0).start()
    for copy in smalls[4:]:
        copy.start()
    for c in range(1, chunks):
        k_copy(c).start()
        v_copy(c).start()
    for i in range(mp):
        w_copy(i).start()

    barrier = pltpu.get_barrier_semaphore()

    def greet_dp(i, carry):
        pl.semaphore_signal(
            barrier, inc=1, device_id=(lax.rem(d + i, n), m), device_id_type=MESH
        )
        return carry

    def greet_mp(i, carry):
        pl.semaphore_signal(
            barrier, inc=1, device_id=(d, lax.rem(m + i, mp)), device_id_type=MESH
        )
        return carry

    lax.fori_loop(1, n, greet_dp, 0)
    lax.fori_loop(1, mp, greet_mp, 0)

    for copy in smalls:
        copy.wait()

    knf[...] = knb[...].astype(F32)
    vnf[...] = vnb[...].astype(F32)
    request = sreq[...]
    high = request // 128
    low_part = request - high * 128
    lane_rows = lax.broadcasted_iota(jnp.int32, (128, slots), 0)
    hot_low = (lane_rows == low_part).astype(F32).astype(BF)
    table = nn_dot(radp[...].astype(F32).astype(BF), hot_low)
    high_rows = lax.broadcasted_iota(jnp.int32, table.shape, 0)
    adapter = jnp.sum(
        jnp.where(high_rows == high, table, 0.0), axis=0, keepdims=True
    ).astype(jnp.int32)
    owner = adapter // 2
    local_id = adapter - owner * 2
    owner_rows = lax.broadcasted_iota(jnp.int32, (n, slots), 0)
    hot_owner = (owner_rows == owner).astype(F32)
    before = (
        lax.broadcasted_iota(jnp.int32, (slots, slots), 0)
        < lax.broadcasted_iota(jnp.int32, (slots, slots), 1)
    ).astype(F32)
    earlier = nn_dot(hot_owner.astype(BF), before.astype(BF))
    position = jnp.sum(hot_owner * earlier, axis=0, keepdims=True).astype(jnp.int32)
    code = owner * cap + position
    code_rows = lax.broadcasted_iota(jnp.int32, (codes, slots), 0)
    hot_code = (code_rows == code).astype(F32)
    disp[...] = hot_code.astype(BF)
    ids = nn_dot(
        (hot_code * local_id.astype(F32)).astype(BF), jnp.ones((slots, 128), BF)
    )
    ids_out[...] = ids.reshape(n, cap, 128).astype(BF)
    same = lax.broadcasted_iota(
        jnp.int32, (slots, slots), 0
    ) == lax.broadcasted_iota(jnp.int32, (slots, slots), 1)
    code_column = jnp.sum(
        jnp.where(same, code.astype(F32), 0.0), axis=1, keepdims=True
    ).astype(jnp.int32)
    comb[...] = (
        (lax.broadcasted_iota(jnp.int32, (slots, codes), 1) == code_column)
        .astype(F32)
        .astype(BF)
    )
    live = jnp.sum(
        jnp.where(same, occ[...].astype(F32), 0.0), axis=1, keepdims=True
    )

    lanes = lax.broadcasted_iota(jnp.int32, (heads, width), 1)

    def attend(c, carry):
        k_copy(c).wait()
        v_copy(c).wait()
        scores, fresh, new_values = [], [], []
        for p in range(CHUNK // 2):
            slot = c * CHUNK + 2 * p
            queries = qbuf[pl.ds(pl.multiple_of(slot * heads, 16), 2 * heads), :]
            keys = kbuf[pl.ds(slot, 2)].reshape(2 * 128, width)
            both = nt_dot(queries, keys) * inverse
            wide = queries.astype(F32)
            for b in range(2):
                tile = both[b * heads : (b + 1) * heads, b * 128 : (b + 1) * 128]
                scores.append(jnp.where(lanes < lens[0, slot + b], tile, -jnp.inf))
                new_key = knf[pl.ds(slot + b, 1), :]
                fresh.append(
                    jnp.sum(
                        wide[b * heads : (b + 1) * heads] * new_key,
                        axis=1,
                        keepdims=True,
                    )
                )
        scores = jnp.concatenate(scores, axis=0)
        fresh = jnp.concatenate(fresh, axis=0) * inverse
        top = jnp.maximum(jnp.max(scores, axis=1, keepdims=True), fresh)
        scores_exp = jnp.exp(scores - top)
        fresh_exp = jnp.exp(fresh - top)
        total = jnp.sum(scores_exp, axis=1, keepdims=True) + fresh_exp
        scale = 1.0 / total
        weights = scores_exp * scale
        fresh_w = (fresh_exp * scale).astype(BF).astype(F32)
        blank = jnp.zeros((heads, 128), F32)
        for p in range(CHUNK // 2):
            slot = c * CHUNK + 2 * p
            r = 2 * p * heads
            pair = jnp.concatenate(
                [
                    jnp.concatenate([weights[r : r + heads], blank], axis=1),
                    jnp.concatenate([blank, weights[r + heads : r + 2 * heads]], axis=1),
                ],
                axis=0,
            ).astype(BF)
            values = vbuf[pl.ds(slot, 2)].reshape(2 * 128, width)
            summed = nn_dot(pair, values)
            for b in range(2):
                new_value = vnf[pl.ds(slot + b, 1), :]
                q = r + b * heads
                obuf[pl.ds(pl.multiple_of((slot + b) * heads, heads), heads), :] = (
                    summed[b * heads : (b + 1) * heads]
                    + fresh_w[q : q + heads] * new_value
                )
        return carry

    first = chunks // 2
    lax.fori_loop(0, first, attend, 0)

    pl.semaphore_wait(barrier, n - 1 + mp - 1)

    def to_owner(out, landing, sems):
        def copy(i):
            peer = lax.rem(d + i, n)
            return pltpu.make_async_remote_copy(
                src_ref=out.at[peer],
                dst_ref=landing.at[d],
                send_sem=sems.at[0, i],
                recv_sem=sems.at[1, i],
                device_id=(peer, m),
                device_id_type=MESH,
            )

        return copy

    def over_mp(out, landing, sems, same_for_all):
        def copy(i):
            peer = lax.rem(m + i, mp)
            return pltpu.make_async_remote_copy(
                src_ref=out if same_for_all else out.at[peer],
                dst_ref=landing.at[m],
                send_sem=sems.at[0, i],
                recv_sem=sems.at[1, i],
                device_id=(d, peer),
                device_id_type=MESH,
            )

        return copy

    def start_all(copy, count):
        def go(i, carry):
            copy(i).start()
            return carry

        lax.fori_loop(1, count, go, 0)

    def recv_all(copy, count):
        def go(i, carry):
            copy(i).wait_recv()
            return carry

        lax.fori_loop(1, count, go, 0)

    def sent_all(copy, count):
        def go(i, carry):
            copy(i).wait_send()
            return carry

        lax.fori_loop(1, count, go, 0)

    ids_copy = to_owner(ids_out, ids_in, ids_sems)
    rows_copy = to_owner(rows_out, rows_in, rows_sems)
    back_copy = to_owner(back_out, back_in, back_sems)
    rs_copy = over_mp(rs_out, rs_in, rs_sems, False)
    ag_copy = over_mp(ag_out, ag_in, ag_sems, True)

    start_all(ids_copy, n)
    lax.fori_loop(first, chunks, attend, 0)
    ids_in[d] = ids_out[d]

    for j in range(heads):
        cols = pl.ds(j * width, width)
        head = obuf[pl.ds(j, slots, stride=heads), :].astype(BF)
        att[:, cols] = head
        sent = nn_dot(disp[...], head)
        rows_out[:, :, cols] = sent.reshape(n, cap, width).astype(BF)
    start_all(rows_copy, n)

    def block_product(i):
        w_copy(i).wait()
        part[i] = nn_dot(att[...], wbuf[i])

    messages = chain_messages(half)
    where = {message: i for i, message in enumerate(messages)}

    def slot_of(direction, left):
        return offsets.index(left if direction == 0 or left in (0, half) else -left)

    def lane_rows_of(direction, lane):
        upper = lane if direction == 0 else 1 - lane
        return pl.ds(upper * side, side)

    def msg_copy(direction, i):
        peer = lax.rem(m + (1 if direction == 0 else mp - 1), mp)
        return pltpu.make_async_remote_copy(
            src_ref=msg_out.at[direction, i],
            dst_ref=msg_in.at[direction, i],
            send_sem=msg_send.at[direction, i],
            recv_sem=msg_recv.at[direction, i],
            device_id=(d, peer),
            device_id_type=MESH,
        )

    def send_message(i):
        left, lane = messages[i]
        for direction in range(2):
            rows = lane_rows_of(direction, lane)
            value = part[slot_of(direction, left), rows, :]
            came = where.get((left + 1, lane))
            if came is not None:
                msg_copy(direction, came).wait_recv()
                value = value + msg_in[direction, came].astype(F32)
            msg_out[direction, i] = value.astype(BF)
            msg_copy(direction, i).start()

    def finish_base():
        for lane in range(2):
            last = where[(1, lane)] if (1, lane) in where else None
            if last is None:
                continue
            for direction in range(2):
                rows = lane_rows_of(direction, lane)
                msg_copy(direction, last).wait_recv()
                base[rows, :] += msg_in[direction, last].astype(F32)

    def share_rows():
        recv_all(ids_copy, n)
        rows_in[d] = rows_out[d]
        recv_all(rows_copy, n)
        got = rows_in[...].astype(F32).reshape(codes, rows_in.shape[2]).astype(BF)
        partial_low = nt_dot(got, shr[...])
        which = ids_in[...].astype(F32).reshape(codes, 128)
        row = lax.broadcasted_iota(jnp.int32, (codes, 128), 0)
        second = ((row // half_group) % 2).astype(F32)
        placed = jnp.where(which == second, partial_low, pltpu.roll(partial_low, 64, 1))
        lane = lax.broadcasted_iota(jnp.int32, (half_group, 128), 1)
        for g in range(mp):
            r = g * group
            rs_out[g] = jnp.where(
                lane < 64,
                placed[r : r + half_group],
                placed[r + half_group : r + group],
            )
        start_all(rs_copy, mp)
        rs_in[m] = rs_out[m]

    def sum_low():
        recv_all(rs_copy, mp)
        ag_out[...] = jnp.sum(rs_in[...], axis=0).astype(BF)
        start_all(ag_copy, mp)
        ag_in[m] = ag_out[...]

    def expand_low():
        recv_all(ag_copy, mp)
        low = ag_in[...].astype(F32)
        twice = jnp.concatenate(
            [low[g] for g in range(mp) for _ in range(2)], axis=0
        )
        which = ids_in[...].astype(F32).reshape(codes, 128)
        row = lax.broadcasted_iota(jnp.int32, (codes, 128), 0)
        second = ((row // half_group) % 2).astype(F32)
        lane_half = (
            lax.broadcasted_iota(jnp.int32, (codes, 128), 1) // 64
        ).astype(F32)
        moved = jnp.where(which == second, twice, pltpu.roll(twice, 64, 1))
        kept = jnp.where(which == lane_half, moved, 0.0).astype(BF)
        delta = 0.5 * nn_dot(kept, expw[...])
        back_out[...] = delta.reshape(n, cap, outw).astype(BF)
        start_all(back_copy, n)
        back_in[d] = back_out[d]

    count = len(messages)
    block_product(0)
    send_message(0)
    block_product(1)
    block_product(2)
    send_message(1)
    block_product(3)
    block_product(4)
    send_message(2)
    block_product(5)
    block_product(6)
    send_message(3)
    w_copy(mp - 1).wait()
    base[...] = nn_dot(att[...], wbuf[mp - 1])
    send_message(4)
    share_rows()
    send_message(5)
    sum_low()
    send_message(6)
    expand_low()
    finish_base()

    recv_all(back_copy, n)
    returned = back_in[...].astype(F32).reshape(codes, outw).astype(BF)
    correction = nn_dot(comb[...], returned)
    out_ref[...] = (live * (base[...] + correction)).astype(BF)

    for copy, total_count in (
        (ids_copy, n),
        (rows_copy, n),
        (back_copy, n),
        (rs_copy, mp),
        (ag_copy, mp),
    ):
        sent_all(copy, total_count)
    for i in range(count):
        for direction in range(2):
            msg_copy(direction, i).wait_send()


def solution(mesh):
    n = mesh.shape["dp"]
    mp = mesh.shape["mp"]

    def body(
        queries,
        key_cache,
        value_cache,
        key_new,
        value_new,
        lengths,
        occupied,
        slot_request,
        request_adapter,
        out_weight,
        shrink_weight,
        expand_weight,
    ):
        slots, heads, width = queries.shape
        cached = key_cache.shape[2]
        features = heads * width
        outw = expand_weight.shape[2]
        cap = 2 * slots // n
        codes = n * cap
        ranks = shrink_weight.shape[0] * shrink_weight.shape[2]
        requests = request_adapter.shape[0]
        chunks = slots // CHUNK
        messages = 2 * (mp // 2) - 1
        packed = codes // mp // 2
        any_spec = pl.BlockSpec(memory_space=pl.ANY)
        dma = pltpu.SemaphoreType.DMA
        return pl.pallas_call(
            functools.partial(kernel, n, mp, cap),
            out_shape=jax.ShapeDtypeStruct((slots, outw), BF),
            in_specs=[any_spec] * 12,
            out_specs=pl.BlockSpec(memory_space=pltpu.VMEM),
            scratch_shapes=[
                pltpu.SMEM((1, slots), jnp.int32),
                pltpu.VMEM((1, slots), jnp.int32),
                pltpu.VMEM((1, slots), jnp.int32),
                pltpu.VMEM((requests // 128, 128), jnp.int32),
                pltpu.VMEM((slots * heads, width), BF),
                pltpu.VMEM((slots, cached, width), BF),
                pltpu.VMEM((slots, cached, width), BF),
                pltpu.VMEM((slots, width), BF),
                pltpu.VMEM((slots, width), BF),
                pltpu.VMEM((slots, width), F32),
                pltpu.VMEM((slots, width), F32),
                pltpu.VMEM((mp, features, outw), BF),
                pltpu.VMEM((ranks, features), BF),
                pltpu.VMEM((ranks, outw), BF),
                pltpu.VMEM((slots * heads, width), F32),
                pltpu.VMEM((slots, features), BF),
                pltpu.VMEM((codes, slots), BF),
                pltpu.VMEM((slots, codes), BF),
                pltpu.VMEM((n, cap, 128), BF),
                pltpu.VMEM((n, cap, 128), BF),
                pltpu.VMEM((n, cap, features), BF),
                pltpu.VMEM((n, cap, features), BF),
                pltpu.VMEM((mp, slots, outw), F32),
                pltpu.VMEM((2, messages, slots // 2, outw), BF),
                pltpu.VMEM((2, messages, slots // 2, outw), BF),
                pltpu.VMEM((slots, outw), F32),
                pltpu.VMEM((mp, packed, 128), F32),
                pltpu.VMEM((mp, packed, 128), F32),
                pltpu.VMEM((packed, 128), BF),
                pltpu.VMEM((mp, packed, 128), BF),
                pltpu.VMEM((n, cap, outw), BF),
                pltpu.VMEM((n, cap, outw), BF),
                dma((9,)),
                dma((chunks,)),
                dma((chunks,)),
                dma((mp,)),
                dma((2, n)),
                dma((2, n)),
                dma((2, mp)),
                dma((2, mp)),
                dma((2, n)),
                dma((2, messages)),
                dma((2, messages)),
            ],
            compiler_params=pltpu.CompilerParams(
                collective_id=0,
                has_side_effects=True,
                vmem_limit_bytes=48 << 20,
            ),
        )(
            lengths.reshape(1, slots),
            occupied.reshape(1, slots),
            slot_request.reshape(1, slots),
            request_adapter.reshape(requests // 128, 128),
            queries.reshape(slots * heads, width),
            key_cache.reshape(slots, cached, width),
            value_cache.reshape(slots, cached, width),
            key_new.reshape(slots, width),
            value_new.reshape(slots, width),
            out_weight,
            shrink_weight.transpose(0, 2, 1).reshape(ranks, features),
            expand_weight.reshape(ranks, outw),
        )

    placed = (
        P("dp", "mp", None),
        P("dp", "mp", None, None),
        P("dp", "mp", None, None),
        P("dp", "mp", None),
        P("dp", "mp", None),
        P("dp"),
        P("dp"),
        P("dp"),
        P(),
        P("mp", None),
        P("dp", "mp", None),
        P("dp", None, "mp"),
    )
    return jax.shard_map(
        body, mesh=mesh, in_specs=placed, out_specs=P("dp", "mp"), check_vma=False
    )
```

```python
import functools
import math

import jax
import jax.numpy as jnp
from jax import lax
from jax.experimental import pallas as pl
from jax.experimental.pallas import tpu as pltpu
from jax.sharding import PartitionSpec as P

MESH = pl.DeviceIdType.MESH
BF = jnp.bfloat16
F32 = jnp.float32


def nt_dot(a, b):
    return lax.dot_general(a, b, (((1,), (1,)), ((), ())), preferred_element_type=F32)


def nn_dot(a, b):
    return jnp.dot(a, b, preferred_element_type=F32)


def chain_messages(half):
    messages = [(half, 0)]
    for left in range(half - 1, 0, -1):
        messages += [(left, 1), (left, 0)]
    return messages


def kernel(
    n,
    mp,
    cap,
    lens_hbm,
    occ_hbm,
    sreq_hbm,
    radp_hbm,
    q_hbm,
    k_hbm,
    v_hbm,
    kn_hbm,
    vn_hbm,
    w_hbm,
    shr_hbm,
    exp_hbm,
    out_ref,
    lens,
    occ,
    sreq,
    radp,
    qbuf,
    kbuf,
    vbuf,
    knb,
    vnb,
    lens_wide,
    wbuf,
    shr,
    expw,
    obuf,
    att,
    disp,
    comb,
    rows_out,
    rows_in,
    part,
    msg_out,
    msg_in,
    base,
    rs_out,
    rs_in,
    ag_out,
    ag_in,
    back_out,
    back_in,
    small_sem,
    k_sem,
    v_sem,
    w_sem,
    rows_sems,
    rs_sems,
    ag_sems,
    back_sems,
    msg_send,
    msg_recv,
):
    d = lax.axis_index("dp")
    m = lax.axis_index("mp")
    slots = lens.shape[1]
    heads = qbuf.shape[0] // slots
    width = qbuf.shape[1]
    outw = expw.shape[1]
    features = heads * width
    codes = n * cap
    group = codes // mp
    half_group = group // 2
    half = mp // 2
    inverse = 1.0 / math.sqrt(width)
    chunk = slots // 2
    chunks = slots // chunk
    fetch = slots // 8
    fetches = slots // fetch
    side = slots // 2

    smalls = [
        pltpu.make_async_copy(src, dst, small_sem.at[i])
        for i, (src, dst) in enumerate(
            [
                (lens_hbm, lens),
                (q_hbm, qbuf),
                (kn_hbm, knb),
                (vn_hbm, vnb),
                (sreq_hbm, sreq),
                (radp_hbm, radp),
                (occ_hbm, occ),
                (shr_hbm, shr),
                (exp_hbm, expw),
            ]
        )
    ]

    def k_copy(c):
        rows = pl.ds(c * fetch, fetch)
        return pltpu.make_async_copy(k_hbm.at[rows], kbuf.at[rows], k_sem.at[c])

    def v_copy(c):
        rows = pl.ds(c * fetch, fetch)
        return pltpu.make_async_copy(v_hbm.at[rows], vbuf.at[rows], v_sem.at[c])

    offsets = [half]
    for r in range(half - 1, 0, -1):
        offsets += [r, -r]
    offsets += [0]

    def w_copy(i):
        block = (m + offsets[i] + mp) % mp
        cols = pl.ds(pl.multiple_of(block * outw, outw), outw)
        return pltpu.make_async_copy(w_hbm.at[:, cols], wbuf.at[i], w_sem.at[i])

    for copy in smalls[:4]:
        copy.start()
    k_copy(0).start()
    v_copy(0).start()
    for copy in smalls[4:]:
        copy.start()
    for c in range(1, fetches):
        k_copy(c).start()
        v_copy(c).start()

    barrier = pltpu.get_barrier_semaphore()

    def greet_dp(i, carry):
        pl.semaphore_signal(
            barrier, inc=1, device_id=((d + i) % n, m), device_id_type=MESH
        )
        return carry

    def greet_mp(i, carry):
        pl.semaphore_signal(
            barrier, inc=1, device_id=(d, (m + i) % mp), device_id_type=MESH
        )
        return carry

    lax.fori_loop(1, n, greet_dp, 0)
    lax.fori_loop(1, mp, greet_mp, 0)

    for copy in smalls:
        copy.wait()

    request = sreq[...]
    high = request // 128
    low_part = request - high * 128
    lane_rows = lax.broadcasted_iota(jnp.int32, (128, slots), 0)
    hot_low = (lane_rows == low_part).astype(F32).astype(BF)
    table = nn_dot(radp[...].astype(F32).astype(BF), hot_low)
    high_rows = lax.broadcasted_iota(jnp.int32, table.shape, 0)
    adapter = jnp.sum(
        jnp.where(high_rows == high, table, 0.0), axis=0, keepdims=True
    ).astype(jnp.int32)
    owner = adapter // 2
    local_id = adapter - owner * 2
    owner_rows = lax.broadcasted_iota(jnp.int32, (n, slots), 0)
    hot_owner = (owner_rows == owner).astype(F32)
    before = (
        lax.broadcasted_iota(jnp.int32, (slots, slots), 0)
        < lax.broadcasted_iota(jnp.int32, (slots, slots), 1)
    ).astype(F32)
    earlier = nn_dot(hot_owner.astype(BF), before.astype(BF))
    position = jnp.sum(hot_owner * earlier, axis=0, keepdims=True).astype(jnp.int32)
    code = owner * cap + position
    code_rows = lax.broadcasted_iota(jnp.int32, (codes, slots), 0)
    hot_code = (code_rows == code).astype(F32)
    disp[...] = hot_code.astype(BF)
    ids = nn_dot(
        (hot_code * local_id.astype(F32)).astype(BF), jnp.ones((slots, 128), BF)
    )
    rows_out[:, :, features:] = ids.reshape(n, cap, 128).astype(BF)
    same = lax.broadcasted_iota(
        jnp.int32, (slots, slots), 0
    ) == lax.broadcasted_iota(jnp.int32, (slots, slots), 1)
    code_column = jnp.sum(
        jnp.where(same, code.astype(F32), 0.0), axis=1, keepdims=True
    ).astype(jnp.int32)
    comb[...] = (
        (lax.broadcasted_iota(jnp.int32, (slots, codes), 1) == code_column)
        .astype(F32)
        .astype(BF)
    )
    live = jnp.sum(
        jnp.where(same, occ[...].astype(F32), 0.0), axis=1, keepdims=True
    )

    span = chunk * heads
    lane_slot = lax.broadcasted_iota(jnp.int32, (chunk, span), 1) // heads
    row_slot = lax.broadcasted_iota(jnp.int32, (chunk, span), 0)
    own = (lane_slot == row_slot).astype(F32)
    positions = lax.broadcasted_iota(jnp.int32, (width, span), 0).astype(F32)
    slot_of_row = lax.broadcasted_iota(jnp.int32, (chunks, slots), 1)
    chunk_of_row = lax.broadcasted_iota(jnp.int32, (chunks, slots), 0)
    in_chunk = (slot_of_row // chunk == chunk_of_row).astype(F32)
    spread = (
        lax.broadcasted_iota(jnp.int32, (slots, span), 0) % chunk
        == lax.broadcasted_iota(jnp.int32, (slots, span), 1) // heads
    ).astype(F32)
    lens_wide[...] = nn_dot(
        (in_chunk * lens[...].astype(F32)).astype(BF), spread.astype(BF)
    )

    def attend(c, carry):
        rows = pl.ds(pl.multiple_of(c * span, span), span)
        first = c * chunk
        for f in range(chunk // fetch):
            k_copy(c * (chunk // fetch) + f).wait()
        tiles = []
        for p in range(chunk // 2):
            pair_rows = pl.ds(pl.multiple_of((first + 2 * p) * heads, 16), 2 * heads)
            keys = kbuf[pl.ds(first + 2 * p, 2)].reshape(2 * width, width)
            both = nt_dot(qbuf[pair_rows, :], keys)
            tiles += [both[:heads, :width], both[heads:, width:]]
        products = jnp.concatenate(tiles, axis=0).T * inverse
        new_keys = knb[pl.ds(pl.multiple_of(first, chunk), chunk), :]
        fresh = jnp.sum(
            own * nt_dot(new_keys, qbuf[rows, :]), axis=0, keepdims=True
        ) * inverse
        scores = jnp.where(
            positions < lens_wide[pl.ds(c, 1), :], products, -jnp.inf
        )
        top = jnp.maximum(jnp.max(scores, axis=0, keepdims=True), fresh)
        scores_exp = jnp.exp(scores - top)
        fresh_exp = jnp.exp(fresh - top)
        total = jnp.sum(scores_exp, axis=0, keepdims=True) + fresh_exp
        scale = 1.0 / total
        weights = (scores_exp * scale).T
        fresh_w = (own * (fresh_exp * scale)).astype(BF)
        new_values = vnb[pl.ds(pl.multiple_of(first, chunk), chunk), :]
        fresh_sum = lax.dot_general(
            fresh_w, new_values, (((0,), (0,)), ((), ())), preferred_element_type=F32
        )
        blank = jnp.zeros((heads, width), F32)
        for f in range(chunk // fetch):
            v_copy(c * (chunk // fetch) + f).wait()
        sums = []
        for p in range(chunk // 2):
            r = 2 * p * heads
            pair = jnp.concatenate(
                [
                    jnp.concatenate([weights[r : r + heads], blank], axis=1),
                    jnp.concatenate([blank, weights[r + heads : r + 2 * heads]], axis=1),
                ],
                axis=0,
            ).astype(BF)
            values = vbuf[pl.ds(first + 2 * p, 2)].reshape(2 * width, width)
            sums.append(nn_dot(pair, values))
        obuf[rows, :] = jnp.concatenate(sums, axis=0) + fresh_sum
        return carry

    attend(0, 0)
    for i in range(mp):
        w_copy(i).start()
    lax.fori_loop(1, chunks, attend, 0)

    class Exchange:
        def __init__(self, out, landing, sems, over_dp, same_for_all=False):
            self.count = n if over_dp else mp
            self.out, self.landing, self.sems = out, landing, sems
            self.over_dp, self.same_for_all = over_dp, same_for_all

        def device(self, i):
            return ((d + i) % n, m) if self.over_dp else (d, (m + i) % mp)

        def start(self):
            here = d if self.over_dp else m
            for i in range(1, self.count):
                device = self.device(i)
                peer = device[0] if self.over_dp else device[1]
                pltpu.make_async_remote_copy(
                    src_ref=self.out if self.same_for_all else self.out.at[peer],
                    dst_ref=self.landing.at[here],
                    send_sem=self.sems.at[0],
                    recv_sem=self.sems.at[1],
                    device_id=device,
                    device_id_type=MESH,
                ).start()

        def whole(self):
            all_blocks = self.landing.at[pl.ds(0, self.count - 1)]
            return pltpu.make_async_remote_copy(
                src_ref=all_blocks,
                dst_ref=all_blocks,
                send_sem=self.sems.at[0],
                recv_sem=self.sems.at[1],
                device_id=self.device(1),
                device_id_type=MESH,
            )

        def arrived(self):
            self.whole().wait_recv()

        def left(self):
            self.whole().wait_send()

    rows_ex = Exchange(rows_out, rows_in, rows_sems, True)
    back_ex = Exchange(back_out, back_in, back_sems, True)
    rs_ex = Exchange(rs_out, rs_in, rs_sems, False)
    ag_ex = Exchange(ag_out, ag_in, ag_sems, False, True)

    pl.semaphore_wait(barrier, n - 1 + mp - 1)

    for j in range(heads):
        cols = pl.ds(j * width, width)
        head = obuf[pl.ds(j, slots, stride=heads), :].astype(BF)
        att[:, cols] = head
        sent = nn_dot(disp[...], head)
        rows_out[:, :, cols] = sent.reshape(n, cap, width).astype(BF)
    rows_ex.start()
    rows_in[d] = rows_out[d]

    def block_product(i):
        w_copy(i).wait()
        part[i] = nn_dot(att[...], wbuf[i])

    messages = chain_messages(half)
    where = {message: i for i, message in enumerate(messages)}

    def slot_of(direction, left):
        return offsets.index(left if direction == 0 or left in (0, half) else -left)

    def lane_rows_of(direction, lane):
        upper = lane if direction == 0 else 1 - lane
        return pl.ds(upper * side, side)

    def msg_copy(direction, i):
        peer = (m + (1 if direction == 0 else mp - 1)) % mp
        return pltpu.make_async_remote_copy(
            src_ref=msg_out.at[direction, i],
            dst_ref=msg_in.at[direction, i],
            send_sem=msg_send.at[0],
            recv_sem=msg_recv.at[direction, i],
            device_id=(d, peer),
            device_id_type=MESH,
        )

    def send_message(i):
        left, lane = messages[i]
        for direction in range(2):
            rows = lane_rows_of(direction, lane)
            value = part[slot_of(direction, left), rows, :]
            came = where.get((left + 1, lane))
            if came is not None:
                msg_copy(direction, came).wait_recv()
                value = value + msg_in[direction, came].astype(F32)
            msg_out[direction, i] = value.astype(BF)
            msg_copy(direction, i).start()

    def finish_base():
        for lane in range(2):
            last = where[(1, lane)] if (1, lane) in where else None
            if last is None:
                continue
            for direction in range(2):
                rows = lane_rows_of(direction, lane)
                msg_copy(direction, last).wait_recv()
                base[rows, :] += msg_in[direction, last].astype(F32)

    def share_rows():
        rows_ex.arrived()
        got = rows_in[:, :, :features].astype(F32).reshape(codes, features).astype(BF)
        partial_low = nt_dot(got, shr[...])
        which = rows_in[:, :, features:].astype(F32).reshape(codes, 128)
        row = lax.broadcasted_iota(jnp.int32, (codes, 128), 0)
        second = ((row // half_group) % 2).astype(F32)
        placed = jnp.where(which == second, partial_low, pltpu.roll(partial_low, 64, 1))
        lane = lax.broadcasted_iota(jnp.int32, (half_group, 128), 1)
        for g in range(mp):
            r = g * group
            rs_out[g] = jnp.where(
                lane < 64,
                placed[r : r + half_group],
                placed[r + half_group : r + group],
            )
        rs_ex.start()
        rs_in[m] = rs_out[m]

    def sum_low():
        rs_ex.arrived()
        ag_out[...] = jnp.sum(rs_in[...], axis=0).astype(BF)
        ag_ex.start()
        ag_in[m] = ag_out[...]

    def expand_low():
        ag_ex.arrived()
        low = ag_in[...].astype(F32)
        twice = jnp.concatenate(
            [low[g] for g in range(mp) for _ in range(2)], axis=0
        )
        which = rows_in[:, :, features:].astype(F32).reshape(codes, 128)
        row = lax.broadcasted_iota(jnp.int32, (codes, 128), 0)
        second = ((row // half_group) % 2).astype(F32)
        lane_half = (
            lax.broadcasted_iota(jnp.int32, (codes, 128), 1) // 64
        ).astype(F32)
        moved = jnp.where(which == second, twice, pltpu.roll(twice, 64, 1))
        kept = jnp.where(which == lane_half, moved, 0.0).astype(BF)
        delta = 0.5 * nn_dot(kept, expw[...])
        back_out[...] = delta.reshape(n, cap, outw).astype(BF)
        back_ex.start()
        back_in[d] = back_out[d]

    block_product(0)
    send_message(0)
    block_product(1)
    block_product(2)
    send_message(1)
    block_product(3)
    block_product(4)
    send_message(2)
    block_product(5)
    block_product(6)
    send_message(3)
    w_copy(mp - 1).wait()
    base[...] = nn_dot(att[...], wbuf[mp - 1])
    send_message(4)
    share_rows()
    send_message(5)
    sum_low()
    send_message(6)
    expand_low()
    finish_base()

    back_ex.arrived()
    returned = back_in[...].astype(F32).reshape(codes, outw).astype(BF)
    correction = nn_dot(comb[...], returned)
    out_ref[...] = (live * (base[...] + correction)).astype(BF)

    for exchange in (rows_ex, back_ex, rs_ex, ag_ex):
        exchange.left()
    pltpu.make_async_remote_copy(
        src_ref=msg_out,
        dst_ref=msg_in,
        send_sem=msg_send.at[0],
        recv_sem=msg_recv.at[0, 0],
        device_id=(d, (m + 1) % mp),
        device_id_type=MESH,
    ).wait_send()


def solution(mesh):
    n = mesh.shape["dp"]
    mp = mesh.shape["mp"]

    def body(
        queries,
        key_cache,
        value_cache,
        key_new,
        value_new,
        lengths,
        occupied,
        slot_request,
        request_adapter,
        out_weight,
        shrink_weight,
        expand_weight,
    ):
        slots, heads, width = queries.shape
        cached = key_cache.shape[2]
        features = heads * width
        outw = expand_weight.shape[2]
        cap = 2 * slots // n
        codes = n * cap
        ranks = shrink_weight.shape[0] * shrink_weight.shape[2]
        requests = request_adapter.shape[0]
        chunk = slots // 2
        chunks = slots // chunk
        fetch = slots // 8
        fetches = slots // fetch
        messages = 2 * (mp // 2) - 1
        packed = codes // mp // 2
        any_spec = pl.BlockSpec(memory_space=pltpu.HBM)
        dma = pltpu.SemaphoreType.DMA
        return pl.pallas_call(
            functools.partial(kernel, n, mp, cap),
            out_shape=pltpu.VMEM((slots, outw), BF),
            in_specs=[any_spec] * 12,
            out_specs=pl.BlockSpec(memory_space=pltpu.VMEM),
            scratch_shapes=[
                pltpu.VMEM((1, slots), jnp.int32),
                pltpu.VMEM((1, slots), jnp.int32),
                pltpu.VMEM((1, slots), jnp.int32),
                pltpu.VMEM((requests // 128, 128), jnp.int32),
                pltpu.VMEM((slots * heads, width), BF),
                pltpu.VMEM((slots, cached, width), BF),
                pltpu.VMEM((slots, cached, width), BF),
                pltpu.VMEM((slots, width), BF),
                pltpu.VMEM((slots, width), BF),
                pltpu.VMEM((chunks, chunk * heads), F32),
                pltpu.VMEM((mp, features, outw), BF),
                pltpu.VMEM((ranks, features), BF),
                pltpu.VMEM((ranks, outw), BF),
                pltpu.VMEM((slots * heads, width), F32),
                pltpu.VMEM((slots, features), BF),
                pltpu.VMEM((codes, slots), BF),
                pltpu.VMEM((slots, codes), BF),
                pltpu.VMEM((n, cap, features + 128), BF),
                pltpu.VMEM((n, cap, features + 128), BF),
                pltpu.VMEM((mp, slots, outw), F32),
                pltpu.VMEM((2, messages, slots // 2, outw), BF),
                pltpu.VMEM((2, messages, slots // 2, outw), BF),
                pltpu.VMEM((slots, outw), F32),
                pltpu.VMEM((mp, packed, 128), F32),
                pltpu.VMEM((mp, packed, 128), F32),
                pltpu.VMEM((packed, 128), BF),
                pltpu.VMEM((mp, packed, 128), BF),
                pltpu.VMEM((n, cap, outw), BF),
                pltpu.VMEM((n, cap, outw), BF),
                dma((9,)),
                dma((fetches,)),
                dma((fetches,)),
                dma((mp,)),
                dma((2,)),
                dma((2,)),
                dma((2,)),
                dma((2,)),
                dma((1,)),
                dma((2, messages)),
            ],
            compiler_params=pltpu.CompilerParams(
                collective_id=0,
                has_side_effects=True,
                vmem_limit_bytes=60 << 20,
            ),
        )(
            lengths.reshape(1, slots),
            occupied.reshape(1, slots),
            slot_request.reshape(1, slots),
            request_adapter.reshape(requests // 128, 128),
            queries.reshape(slots * heads, width),
            key_cache.reshape(slots, cached, width),
            value_cache.reshape(slots, cached, width),
            key_new.reshape(slots, width),
            value_new.reshape(slots, width),
            out_weight,
            shrink_weight.transpose(0, 2, 1).reshape(ranks, features),
            expand_weight.reshape(ranks, outw),
        )

    placed = (
        P("dp", "mp", None),
        P("dp", "mp", None, None),
        P("dp", "mp", None, None),
        P("dp", "mp", None),
        P("dp", "mp", None),
        P("dp"),
        P("dp"),
        P("dp"),
        P(),
        P("mp", None),
        P("dp", "mp", None),
        P("dp", None, "mp"),
    )
    return jax.shard_map(
        body, mesh=mesh, in_specs=placed, out_specs=P("dp", "mp"), check_vma=False
    )
```

```python
import functools
import math

import jax
import jax.numpy as jnp
from jax import lax
from jax.experimental import pallas as pl
from jax.experimental.pallas import tpu as pltpu
from jax.sharding import PartitionSpec as P

MESH = pl.DeviceIdType.MESH
BF = jnp.bfloat16
F32 = jnp.float32


def nt_dot(a, b):
    return lax.dot_general(a, b, (((1,), (1,)), ((), ())), preferred_element_type=F32)


def nn_dot(a, b):
    return jnp.dot(a, b, preferred_element_type=F32)


def chain_messages(half):
    messages = [(half, 0)]
    for left in range(half - 1, 0, -1):
        messages += [(left, 1), (left, 0)]
    return messages


def kernel(
    n,
    mp,
    cap,
    lens_hbm,
    occ_hbm,
    sreq_hbm,
    radp_hbm,
    q_hbm,
    k_hbm,
    v_hbm,
    kn_hbm,
    vn_hbm,
    w_hbm,
    shr_hbm,
    exp_hbm,
    out_ref,
    lens,
    occ,
    sreq,
    radp,
    qbuf,
    kbuf,
    vbuf,
    knb,
    vnb,
    lens_wide,
    wbuf,
    shr,
    expw,
    obuf,
    att,
    disp,
    comb,
    rows_out,
    rows_in,
    part,
    msg_out,
    msg_in,
    base,
    rs_out,
    rs_in,
    ag_out,
    ag_in,
    back_out,
    back_in,
    small_sem,
    k_sem,
    v_sem,
    w_sem,
    rows_sems,
    rs_sems,
    ag_sems,
    back_sems,
    msg_send,
    msg_recv,
):
    d = lax.axis_index("dp")
    m = lax.axis_index("mp")
    slots = lens.shape[1]
    heads = qbuf.shape[0] // slots
    width = qbuf.shape[1]
    outw = expw.shape[1]
    features = heads * width
    codes = n * cap
    group = codes // mp
    half_group = group // 2
    half = mp // 2
    inverse = 1.0 / math.sqrt(width)
    chunk = slots
    chunks = slots // chunk
    fetch = slots // 8
    fetches = slots // fetch
    side = slots // 2

    smalls = [
        pltpu.make_async_copy(src, dst, small_sem.at[i])
        for i, (src, dst) in enumerate(
            [
                (lens_hbm, lens),
                (q_hbm, qbuf),
                (kn_hbm, knb),
                (vn_hbm, vnb),
                (sreq_hbm, sreq),
                (radp_hbm, radp),
                (occ_hbm, occ),
                (shr_hbm, shr),
                (exp_hbm, expw),
            ]
        )
    ]

    def k_copy(c):
        rows = pl.ds(c * fetch, fetch)
        return pltpu.make_async_copy(k_hbm.at[rows], kbuf.at[rows], k_sem.at[c])

    def v_copy(c):
        rows = pl.ds(c * fetch, fetch)
        return pltpu.make_async_copy(v_hbm.at[rows], vbuf.at[rows], v_sem.at[c])

    offsets = [half]
    for r in range(half - 1, 0, -1):
        offsets += [r, -r]
    offsets += [0]

    def w_copy(i):
        block = (m + offsets[i] + mp) % mp
        cols = pl.ds(pl.multiple_of(block * outw, outw), outw)
        return pltpu.make_async_copy(w_hbm.at[:, cols], wbuf.at[i], w_sem.at[i])

    for copy in smalls[:4]:
        copy.start()
    for c in range(fetches):
        k_copy(c).start()
    for copy in smalls[4:]:
        copy.start()
    for c in range(fetches):
        v_copy(c).start()

    barrier = pltpu.get_barrier_semaphore()

    def greet_dp(i, carry):
        pl.semaphore_signal(
            barrier, inc=1, device_id=((d + i) % n, m), device_id_type=MESH
        )
        return carry

    def greet_mp(i, carry):
        pl.semaphore_signal(
            barrier, inc=1, device_id=(d, (m + i) % mp), device_id_type=MESH
        )
        return carry

    lax.fori_loop(1, n, greet_dp, 0)
    lax.fori_loop(1, mp, greet_mp, 0)

    for copy in smalls:
        copy.wait()

    request = sreq[...]
    high = request // 128
    low_part = request - high * 128
    lane_rows = lax.broadcasted_iota(jnp.int32, (128, slots), 0)
    hot_low = (lane_rows == low_part).astype(F32).astype(BF)
    table = nn_dot(radp[...].astype(F32).astype(BF), hot_low)
    high_rows = lax.broadcasted_iota(jnp.int32, table.shape, 0)
    adapter = jnp.sum(
        jnp.where(high_rows == high, table, 0.0), axis=0, keepdims=True
    ).astype(jnp.int32)
    owner = adapter // 2
    local_id = adapter - owner * 2
    owner_rows = lax.broadcasted_iota(jnp.int32, (n, slots), 0)
    hot_owner = (owner_rows == owner).astype(F32)
    before = (
        lax.broadcasted_iota(jnp.int32, (slots, slots), 0)
        < lax.broadcasted_iota(jnp.int32, (slots, slots), 1)
    ).astype(F32)
    earlier = nn_dot(hot_owner.astype(BF), before.astype(BF))
    position = jnp.sum(hot_owner * earlier, axis=0, keepdims=True).astype(jnp.int32)
    code = owner * cap + position
    code_rows = lax.broadcasted_iota(jnp.int32, (codes, slots), 0)
    hot_code = (code_rows == code).astype(F32)
    disp[...] = hot_code.astype(BF)
    ids = nn_dot(
        (hot_code * local_id.astype(F32)).astype(BF), jnp.ones((slots, 128), BF)
    )
    rows_out[:, :, features:] = ids.reshape(n, cap, 128).astype(BF)
    same = lax.broadcasted_iota(
        jnp.int32, (slots, slots), 0
    ) == lax.broadcasted_iota(jnp.int32, (slots, slots), 1)
    code_column = jnp.sum(
        jnp.where(same, code.astype(F32), 0.0), axis=1, keepdims=True
    ).astype(jnp.int32)
    comb[...] = (
        (lax.broadcasted_iota(jnp.int32, (slots, codes), 1) == code_column)
        .astype(F32)
        .astype(BF)
    )
    live = jnp.sum(
        jnp.where(same, occ[...].astype(F32), 0.0), axis=1, keepdims=True
    )

    span = chunk * heads
    lane_slot = lax.broadcasted_iota(jnp.int32, (chunk, span), 1) // heads
    row_slot = lax.broadcasted_iota(jnp.int32, (chunk, span), 0)
    own = (lane_slot == row_slot).astype(F32)
    positions = lax.broadcasted_iota(jnp.int32, (width, span), 0).astype(F32)
    slot_of_row = lax.broadcasted_iota(jnp.int32, (chunks, slots), 1)
    chunk_of_row = lax.broadcasted_iota(jnp.int32, (chunks, slots), 0)
    in_chunk = (slot_of_row // chunk == chunk_of_row).astype(F32)
    spread = (
        lax.broadcasted_iota(jnp.int32, (slots, span), 0) % chunk
        == lax.broadcasted_iota(jnp.int32, (slots, span), 1) // heads
    ).astype(F32)
    lens_wide[...] = nn_dot(
        (in_chunk * lens[...].astype(F32)).astype(BF), spread.astype(BF)
    )

    def attend(c, carry):
        rows = pl.ds(pl.multiple_of(c * span, span), span)
        first = c * chunk
        for f in range(chunk // fetch):
            k_copy(c * (chunk // fetch) + f).wait()
        tiles = []
        for p in range(chunk // 2):
            pair_rows = pl.ds(pl.multiple_of((first + 2 * p) * heads, 16), 2 * heads)
            keys = kbuf[pl.ds(first + 2 * p, 2)].reshape(2 * width, width)
            both = nt_dot(qbuf[pair_rows, :], keys)
            tiles += [both[:heads, :width], both[heads:, width:]]
        products = jnp.concatenate(tiles, axis=0).T * inverse
        new_keys = knb[pl.ds(pl.multiple_of(first, chunk), chunk), :]
        fresh = jnp.sum(
            own * nt_dot(new_keys, qbuf[rows, :]), axis=0, keepdims=True
        ) * inverse
        scores = jnp.where(
            positions < lens_wide[pl.ds(c, 1), :], products, -jnp.inf
        )
        top = jnp.maximum(jnp.max(scores, axis=0, keepdims=True), fresh)
        scores_exp = jnp.exp(scores - top)
        fresh_exp = jnp.exp(fresh - top)
        total = jnp.sum(scores_exp, axis=0, keepdims=True) + fresh_exp
        scale = 1.0 / total
        weights = (scores_exp * scale).T
        fresh_w = (own * (fresh_exp * scale)).astype(BF)
        new_values = vnb[pl.ds(pl.multiple_of(first, chunk), chunk), :]
        fresh_sum = lax.dot_general(
            fresh_w, new_values, (((0,), (0,)), ((), ())), preferred_element_type=F32
        )
        blank = jnp.zeros((heads, width), F32)
        for i in range(mp):
            w_copy(i).start()
        for f in range(chunk // fetch):
            v_copy(c * (chunk // fetch) + f).wait()
        sums = []
        for p in range(chunk // 2):
            r = 2 * p * heads
            pair = jnp.concatenate(
                [
                    jnp.concatenate([weights[r : r + heads], blank], axis=1),
                    jnp.concatenate([blank, weights[r + heads : r + 2 * heads]], axis=1),
                ],
                axis=0,
            ).astype(BF)
            values = vbuf[pl.ds(first + 2 * p, 2)].reshape(2 * width, width)
            sums.append(nn_dot(pair, values))
        obuf[rows, :] = jnp.concatenate(sums, axis=0) + fresh_sum
        return carry

    attend(0, 0)

    ring = math.isqrt(n // 2)

    def peer_of(i):
        dx, dy, dc = i // (2 * ring), (i // 2) % ring, i % 2
        x = (d // (2 * ring) + dx) % ring
        y = ((d // 2) % ring + dy) % ring
        return (x * ring + y) * 2 + (d + dc) % 2

    def hops(i):
        dx, dy = i // (2 * ring), (i // 2) % ring
        return min(dx, ring - dx) + min(dy, ring - dy)

    far_first_dp = sorted(range(1, n), key=lambda i: -hops(i))
    far_first_mp = sorted(range(1, mp), key=lambda i: -min(i, mp - i))

    class Exchange:
        def __init__(self, out, landing, sems, over_dp, same_for_all=False):
            self.count = n if over_dp else mp
            self.out, self.landing, self.sems = out, landing, sems
            self.over_dp, self.same_for_all = over_dp, same_for_all

        def device(self, i):
            if not self.over_dp:
                return (d, (m + i) % mp)
            return (peer_of(i), m)

        def start(self):
            here = d if self.over_dp else m
            for i in far_first_dp if self.over_dp else far_first_mp:
                device = self.device(i)
                peer = device[0] if self.over_dp else device[1]
                pltpu.make_async_remote_copy(
                    src_ref=self.out if self.same_for_all else self.out.at[peer],
                    dst_ref=self.landing.at[here],
                    send_sem=self.sems.at[0],
                    recv_sem=self.sems.at[1],
                    device_id=device,
                    device_id_type=MESH,
                ).start()

        def whole(self):
            all_blocks = self.landing.at[pl.ds(0, self.count - 1)]
            return pltpu.make_async_remote_copy(
                src_ref=all_blocks,
                dst_ref=all_blocks,
                send_sem=self.sems.at[0],
                recv_sem=self.sems.at[1],
                device_id=self.device(1),
                device_id_type=MESH,
            )

        def arrived(self):
            self.whole().wait_recv()

        def left(self):
            self.whole().wait_send()

    rows_ex = Exchange(rows_out, rows_in, rows_sems, True)
    back_ex = Exchange(back_out, back_in, back_sems, True)
    rs_ex = Exchange(rs_out, rs_in, rs_sems, False)
    ag_ex = Exchange(ag_out, ag_in, ag_sems, False, True)

    pl.semaphore_wait(barrier, n - 1 + mp - 1)

    for j in range(heads):
        cols = pl.ds(j * width, width)
        head = obuf[pl.ds(j, slots, stride=heads), :].astype(BF)
        att[:, cols] = head
        sent = nn_dot(disp[...], head)
        rows_out[:, :, cols] = sent.reshape(n, cap, width).astype(BF)
    rows_ex.start()
    rows_in[d] = rows_out[d]

    def block_product(i):
        w_copy(i).wait()
        part[i] = nn_dot(att[...], wbuf[i])

    messages = chain_messages(half)
    where = {message: i for i, message in enumerate(messages)}

    def slot_of(direction, left):
        return offsets.index(left if direction == 0 or left in (0, half) else -left)

    def lane_rows_of(direction, lane):
        upper = lane if direction == 0 else 1 - lane
        return pl.ds(upper * side, side)

    def msg_copy(direction, i):
        peer = (m + (1 if direction == 0 else mp - 1)) % mp
        return pltpu.make_async_remote_copy(
            src_ref=msg_out.at[direction, i],
            dst_ref=msg_in.at[direction, i],
            send_sem=msg_send.at[0],
            recv_sem=msg_recv.at[direction, i],
            device_id=(d, peer),
            device_id_type=MESH,
        )

    def send_message(i):
        left, lane = messages[i]
        for direction in range(2):
            rows = lane_rows_of(direction, lane)
            value = part[slot_of(direction, left), rows, :]
            came = where.get((left + 1, lane))
            if came is not None:
                msg_copy(direction, came).wait_recv()
                value = value + msg_in[direction, came].astype(F32)
            msg_out[direction, i] = value.astype(BF)
            msg_copy(direction, i).start()

    def finish_base():
        for lane in range(2):
            last = where[(1, lane)] if (1, lane) in where else None
            if last is None:
                continue
            for direction in range(2):
                rows = lane_rows_of(direction, lane)
                msg_copy(direction, last).wait_recv()
                base[rows, :] += msg_in[direction, last].astype(F32)

    def share_rows():
        rows_ex.arrived()
        got = rows_in[:, :, :features].astype(F32).reshape(codes, features).astype(BF)
        partial_low = nt_dot(got, shr[...])
        which = rows_in[:, :, features:].astype(F32).reshape(codes, 128)
        row = lax.broadcasted_iota(jnp.int32, (codes, 128), 0)
        second = ((row // half_group) % 2).astype(F32)
        placed = jnp.where(which == second, partial_low, pltpu.roll(partial_low, 64, 1))
        lane = lax.broadcasted_iota(jnp.int32, (half_group, 128), 1)
        for g in range(mp):
            r = g * group
            rs_out[g] = jnp.where(
                lane < 64,
                placed[r : r + half_group],
                placed[r + half_group : r + group],
            )
        rs_ex.start()
        rs_in[m] = rs_out[m]

    def sum_low():
        rs_ex.arrived()
        ag_out[...] = jnp.sum(rs_in[...], axis=0).astype(BF)
        ag_ex.start()
        ag_in[m] = ag_out[...]

    def expand_low():
        ag_ex.arrived()
        low = ag_in[...].astype(F32)
        twice = jnp.concatenate(
            [low[g] for g in range(mp) for _ in range(2)], axis=0
        )
        which = rows_in[:, :, features:].astype(F32).reshape(codes, 128)
        row = lax.broadcasted_iota(jnp.int32, (codes, 128), 0)
        second = ((row // half_group) % 2).astype(F32)
        lane_half = (
            lax.broadcasted_iota(jnp.int32, (codes, 128), 1) // 64
        ).astype(F32)
        moved = jnp.where(which == second, twice, pltpu.roll(twice, 64, 1))
        kept = jnp.where(which == lane_half, moved, 0.0).astype(BF)
        delta = 0.5 * nn_dot(kept, expw[...])
        back_out[...] = delta.reshape(n, cap, outw).astype(BF)
        back_ex.start()
        back_in[d] = back_out[d]

    block_product(0)
    send_message(0)
    block_product(1)
    block_product(2)
    send_message(1)
    for i in range(3, mp - 1):
        block_product(i)
    w_copy(mp - 1).wait()
    base[...] = nn_dot(att[...], wbuf[mp - 1])
    send_message(2)
    send_message(3)
    share_rows()
    send_message(4)
    send_message(5)
    sum_low()
    send_message(6)
    expand_low()
    finish_base()

    back_ex.arrived()
    returned = back_in[...].astype(F32).reshape(codes, outw).astype(BF)
    correction = nn_dot(comb[...], returned)
    out_ref[...] = (live * (base[...] + correction)).astype(BF)

    for exchange in (rows_ex, back_ex, rs_ex, ag_ex):
        exchange.left()
    pltpu.make_async_remote_copy(
        src_ref=msg_out,
        dst_ref=msg_in,
        send_sem=msg_send.at[0],
        recv_sem=msg_recv.at[0, 0],
        device_id=(d, (m + 1) % mp),
        device_id_type=MESH,
    ).wait_send()


def solution(mesh):
    n = mesh.shape["dp"]
    mp = mesh.shape["mp"]

    def body(
        queries,
        key_cache,
        value_cache,
        key_new,
        value_new,
        lengths,
        occupied,
        slot_request,
        request_adapter,
        out_weight,
        shrink_weight,
        expand_weight,
    ):
        slots, heads, width = queries.shape
        cached = key_cache.shape[2]
        features = heads * width
        outw = expand_weight.shape[2]
        cap = 2 * slots // n
        codes = n * cap
        ranks = shrink_weight.shape[0] * shrink_weight.shape[2]
        requests = request_adapter.shape[0]
        chunk = slots
        chunks = slots // chunk
        fetch = slots // 8
        fetches = slots // fetch
        messages = 2 * (mp // 2) - 1
        packed = codes // mp // 2
        any_spec = pl.BlockSpec(memory_space=pltpu.HBM)
        dma = pltpu.SemaphoreType.DMA
        return pl.pallas_call(
            functools.partial(kernel, n, mp, cap),
            out_shape=pltpu.VMEM((slots, outw), BF),
            in_specs=[any_spec] * 12,
            out_specs=pl.BlockSpec(memory_space=pltpu.VMEM),
            scratch_shapes=[
                pltpu.VMEM((1, slots), jnp.int32),
                pltpu.VMEM((1, slots), jnp.int32),
                pltpu.VMEM((1, slots), jnp.int32),
                pltpu.VMEM((requests // 128, 128), jnp.int32),
                pltpu.VMEM((slots * heads, width), BF),
                pltpu.VMEM((slots, cached, width), BF),
                pltpu.VMEM((slots, cached, width), BF),
                pltpu.VMEM((slots, width), BF),
                pltpu.VMEM((slots, width), BF),
                pltpu.VMEM((chunks, chunk * heads), F32),
                pltpu.VMEM((mp, features, outw), BF),
                pltpu.VMEM((ranks, features), BF),
                pltpu.VMEM((ranks, outw), BF),
                pltpu.VMEM((slots * heads, width), F32),
                pltpu.VMEM((slots, features), BF),
                pltpu.VMEM((codes, slots), BF),
                pltpu.VMEM((slots, codes), BF),
                pltpu.VMEM((n, cap, features + 128), BF),
                pltpu.VMEM((n, cap, features + 128), BF),
                pltpu.VMEM((mp, slots, outw), F32),
                pltpu.VMEM((2, messages, slots // 2, outw), BF),
                pltpu.VMEM((2, messages, slots // 2, outw), BF),
                pltpu.VMEM((slots, outw), F32),
                pltpu.VMEM((mp, packed, 128), F32),
                pltpu.VMEM((mp, packed, 128), F32),
                pltpu.VMEM((packed, 128), BF),
                pltpu.VMEM((mp, packed, 128), BF),
                pltpu.VMEM((n, cap, outw), BF),
                pltpu.VMEM((n, cap, outw), BF),
                dma((9,)),
                dma((fetches,)),
                dma((fetches,)),
                dma((mp,)),
                dma((2,)),
                dma((2,)),
                dma((2,)),
                dma((2,)),
                dma((1,)),
                dma((2, messages)),
            ],
            compiler_params=pltpu.CompilerParams(
                collective_id=0,
                has_side_effects=True,
                vmem_limit_bytes=60 << 20,
            ),
        )(
            lengths.reshape(1, slots),
            occupied.reshape(1, slots),
            slot_request.reshape(1, slots),
            request_adapter.reshape(requests // 128, 128),
            queries.reshape(slots * heads, width),
            key_cache.reshape(slots, cached, width),
            value_cache.reshape(slots, cached, width),
            key_new.reshape(slots, width),
            value_new.reshape(slots, width),
            out_weight,
            shrink_weight.transpose(0, 2, 1).reshape(ranks, features),
            expand_weight.reshape(ranks, outw),
        )

    placed = (
        P("dp", "mp", None),
        P("dp", "mp", None, None),
        P("dp", "mp", None, None),
        P("dp", "mp", None),
        P("dp", "mp", None),
        P("dp"),
        P("dp"),
        P("dp"),
        P(),
        P("mp", None),
        P("dp", "mp", None),
        P("dp", None, "mp"),
    )
    return jax.shard_map(
        body, mesh=mesh, in_specs=placed, out_specs=P("dp", "mp"), check_vma=False
    )
```

```python
import functools
import math

import jax
import jax.numpy as jnp
from jax import lax
from jax.experimental import pallas as pl
from jax.experimental.pallas import tpu as pltpu
from jax.sharding import PartitionSpec as P

MESH = pl.DeviceIdType.MESH
BF = jnp.bfloat16
F32 = jnp.float32


def nt_dot(a, b):
    return lax.dot_general(a, b, (((1,), (1,)), ((), ())), preferred_element_type=F32)


def nn_dot(a, b):
    return jnp.dot(a, b, preferred_element_type=F32)


def chain_messages(half):
    messages = [(half, 0)]
    for left in range(half - 1, 0, -1):
        messages += [(left, 1), (left, 0)]
    return messages


def kernel(
    n,
    mp,
    cap,
    lens_hbm,
    occ_hbm,
    sreq_hbm,
    radp_hbm,
    q_hbm,
    k_hbm,
    v_hbm,
    kn_hbm,
    vn_hbm,
    w_hbm,
    shr_hbm,
    exp_hbm,
    out_ref,
    lens,
    occ,
    sreq,
    radp,
    qbuf,
    kbuf,
    vbuf,
    knb,
    vnb,
    lens_wide,
    wbuf,
    shr,
    expw,
    obuf,
    att,
    disp,
    comb,
    rows_out,
    rows_in,
    part,
    msg_out,
    msg_in,
    base,
    rs_out,
    rs_in,
    ag_out,
    ag_in,
    back_out,
    back_in,
    small_sem,
    k_sem,
    v_sem,
    w_sem,
    rows_sems,
    rs_sems,
    ag_send,
    ag_recv,
    back_sems,
    msg_send,
    msg_recv,
):
    d = lax.axis_index("dp")
    m = lax.axis_index("mp")
    slots = lens.shape[1]
    heads = qbuf.shape[0] // slots
    width = qbuf.shape[1]
    outw = expw.shape[1]
    features = heads * width
    codes = n * cap
    group = codes // mp
    half_group = group // 2
    half = mp // 2
    inverse = 1.0 / math.sqrt(width)
    chunk = slots
    chunks = slots // chunk
    fetch = slots // 8
    fetches = slots // fetch
    side = slots // 2

    smalls = [
        pltpu.make_async_copy(src, dst, small_sem.at[i])
        for i, (src, dst) in enumerate(
            [
                (lens_hbm, lens),
                (q_hbm, qbuf),
                (kn_hbm, knb),
                (vn_hbm, vnb),
                (sreq_hbm, sreq),
                (radp_hbm, radp),
                (occ_hbm, occ),
                (shr_hbm, shr),
                (exp_hbm, expw),
            ]
        )
    ]

    def k_copy(c):
        rows = pl.ds(c * fetch, fetch)
        return pltpu.make_async_copy(k_hbm.at[rows], kbuf.at[rows], k_sem.at[c])

    def v_copy(c):
        rows = pl.ds(c * fetch, fetch)
        return pltpu.make_async_copy(v_hbm.at[rows], vbuf.at[rows], v_sem.at[c])

    offsets = [half]
    for r in range(half - 1, 0, -1):
        offsets += [r, -r]
    offsets += [0]

    def w_copy(i):
        block = (m + offsets[i] + mp) % mp
        cols = pl.ds(pl.multiple_of(block * outw, outw), outw)
        return pltpu.make_async_copy(w_hbm.at[:, cols], wbuf.at[i], w_sem.at[i])

    for copy in smalls[:4]:
        copy.start()
    for c in range(fetches):
        k_copy(c).start()
    for copy in smalls[4:]:
        copy.start()
    for c in range(fetches):
        v_copy(c).start()

    barrier = pltpu.get_barrier_semaphore()

    def greet_dp(i, carry):
        pl.semaphore_signal(
            barrier, inc=1, device_id=((d + i) % n, m), device_id_type=MESH
        )
        return carry

    def greet_mp(i, carry):
        pl.semaphore_signal(
            barrier, inc=1, device_id=(d, (m + i) % mp), device_id_type=MESH
        )
        return carry

    lax.fori_loop(1, n, greet_dp, 0)
    lax.fori_loop(1, mp, greet_mp, 0)

    for copy in smalls:
        copy.wait()

    request = sreq[...]
    high = request // 128
    low_part = request - high * 128
    lane_rows = lax.broadcasted_iota(jnp.int32, (128, slots), 0)
    hot_low = (lane_rows == low_part).astype(F32).astype(BF)
    table = nn_dot(radp[...].astype(F32).astype(BF), hot_low)
    high_rows = lax.broadcasted_iota(jnp.int32, table.shape, 0)
    adapter = jnp.sum(
        jnp.where(high_rows == high, table, 0.0), axis=0, keepdims=True
    ).astype(jnp.int32)
    owner = adapter // 2
    local_id = adapter - owner * 2
    owner_rows = lax.broadcasted_iota(jnp.int32, (n, slots), 0)
    hot_owner = (owner_rows == owner).astype(F32)
    before = (
        lax.broadcasted_iota(jnp.int32, (slots, slots), 0)
        < lax.broadcasted_iota(jnp.int32, (slots, slots), 1)
    ).astype(F32)
    earlier = nn_dot(hot_owner.astype(BF), before.astype(BF))
    position = jnp.sum(hot_owner * earlier, axis=0, keepdims=True).astype(jnp.int32)
    code = owner * cap + position
    code_rows = lax.broadcasted_iota(jnp.int32, (codes, slots), 0)
    hot_code = (code_rows == code).astype(F32)
    disp[...] = hot_code.astype(BF)
    ids = nn_dot(
        (hot_code * local_id.astype(F32)).astype(BF), jnp.ones((slots, 128), BF)
    )
    rows_out[:, :, features:] = ids.reshape(n, cap, 128).astype(BF)
    same = lax.broadcasted_iota(
        jnp.int32, (slots, slots), 0
    ) == lax.broadcasted_iota(jnp.int32, (slots, slots), 1)
    code_column = jnp.sum(
        jnp.where(same, code.astype(F32), 0.0), axis=1, keepdims=True
    ).astype(jnp.int32)
    comb[...] = (
        (lax.broadcasted_iota(jnp.int32, (slots, codes), 1) == code_column)
        .astype(F32)
        .astype(BF)
    )
    live = jnp.sum(
        jnp.where(same, occ[...].astype(F32), 0.0), axis=1, keepdims=True
    )

    span = chunk * heads
    lane_slot = lax.broadcasted_iota(jnp.int32, (chunk, span), 1) // heads
    row_slot = lax.broadcasted_iota(jnp.int32, (chunk, span), 0)
    own = (lane_slot == row_slot).astype(F32)
    positions = lax.broadcasted_iota(jnp.int32, (width, span), 0).astype(F32)
    slot_of_row = lax.broadcasted_iota(jnp.int32, (chunks, slots), 1)
    chunk_of_row = lax.broadcasted_iota(jnp.int32, (chunks, slots), 0)
    in_chunk = (slot_of_row // chunk == chunk_of_row).astype(F32)
    spread = (
        lax.broadcasted_iota(jnp.int32, (slots, span), 0) % chunk
        == lax.broadcasted_iota(jnp.int32, (slots, span), 1) // heads
    ).astype(F32)
    lens_wide[...] = nn_dot(
        (in_chunk * lens[...].astype(F32)).astype(BF), spread.astype(BF)
    )

    def attend(c, carry):
        rows = pl.ds(pl.multiple_of(c * span, span), span)
        first = c * chunk
        for f in range(chunk // fetch):
            k_copy(c * (chunk // fetch) + f).wait()
        tiles = []
        for p in range(chunk // 2):
            pair_rows = pl.ds(pl.multiple_of((first + 2 * p) * heads, 16), 2 * heads)
            keys = kbuf[pl.ds(first + 2 * p, 2)].reshape(2 * width, width)
            both = nt_dot(qbuf[pair_rows, :], keys)
            tiles += [both[:heads, :width], both[heads:, width:]]
        products = jnp.concatenate(tiles, axis=0).T * inverse
        new_keys = knb[pl.ds(pl.multiple_of(first, chunk), chunk), :]
        fresh = jnp.sum(
            own * nt_dot(new_keys, qbuf[rows, :]), axis=0, keepdims=True
        ) * inverse
        scores = jnp.where(
            positions < lens_wide[pl.ds(c, 1), :], products, -jnp.inf
        )
        top = jnp.maximum(jnp.max(scores, axis=0, keepdims=True), fresh)
        scores_exp = jnp.exp(scores - top)
        fresh_exp = jnp.exp(fresh - top)
        total = jnp.sum(scores_exp, axis=0, keepdims=True) + fresh_exp
        scale = 1.0 / total
        weights = (scores_exp * scale).T
        fresh_w = (own * (fresh_exp * scale)).astype(BF)
        new_values = vnb[pl.ds(pl.multiple_of(first, chunk), chunk), :]
        fresh_sum = lax.dot_general(
            fresh_w, new_values, (((0,), (0,)), ((), ())), preferred_element_type=F32
        )
        blank = jnp.zeros((heads, width), F32)
        for i in range(mp):
            w_copy(i).start()
        for f in range(chunk // fetch):
            v_copy(c * (chunk // fetch) + f).wait()
        sums = []
        for p in range(chunk // 2):
            r = 2 * p * heads
            pair = jnp.concatenate(
                [
                    jnp.concatenate([weights[r : r + heads], blank], axis=1),
                    jnp.concatenate([blank, weights[r + heads : r + 2 * heads]], axis=1),
                ],
                axis=0,
            ).astype(BF)
            values = vbuf[pl.ds(first + 2 * p, 2)].reshape(2 * width, width)
            sums.append(nn_dot(pair, values))
        obuf[rows, :] = jnp.concatenate(sums, axis=0) + fresh_sum
        return carry

    attend(0, 0)

    ring = math.isqrt(n // 2)

    def peer_of(i):
        dx, dy, dc = i // (2 * ring), (i // 2) % ring, i % 2
        x = (d // (2 * ring) + dx) % ring
        y = ((d // 2) % ring + dy) % ring
        return (x * ring + y) * 2 + (d + dc) % 2

    def hops(i):
        dx, dy = i // (2 * ring), (i // 2) % ring
        return min(dx, ring - dx) + min(dy, ring - dy)

    far_first_dp = sorted(range(1, n), key=lambda i: -hops(i))
    far_first_mp = sorted(range(1, mp), key=lambda i: -min(i, mp - i))

    class Exchange:
        def __init__(self, out, landing, sems, over_dp, same_for_all=False):
            self.count = n if over_dp else mp
            self.out, self.landing, self.sems = out, landing, sems
            self.over_dp, self.same_for_all = over_dp, same_for_all

        def device(self, i):
            if not self.over_dp:
                return (d, (m + i) % mp)
            return (peer_of(i), m)

        def start(self):
            here = d if self.over_dp else m
            for i in far_first_dp if self.over_dp else far_first_mp:
                device = self.device(i)
                peer = device[0] if self.over_dp else device[1]
                pltpu.make_async_remote_copy(
                    src_ref=self.out if self.same_for_all else self.out.at[peer],
                    dst_ref=self.landing.at[here],
                    send_sem=self.sems.at[0],
                    recv_sem=self.sems.at[1],
                    device_id=device,
                    device_id_type=MESH,
                ).start()

        def whole(self):
            all_blocks = self.landing.at[pl.ds(0, self.count - 1)]
            return pltpu.make_async_remote_copy(
                src_ref=all_blocks,
                dst_ref=all_blocks,
                send_sem=self.sems.at[0],
                recv_sem=self.sems.at[1],
                device_id=self.device(1),
                device_id_type=MESH,
            )

        def arrived(self):
            self.whole().wait_recv()

        def left(self):
            self.whole().wait_send()

    rows_ex = Exchange(rows_out, rows_in, rows_sems, True)
    back_ex = Exchange(back_out, back_in, back_sems, True)
    rs_ex = Exchange(rs_out, rs_in, rs_sems, False)

    def low_copy(i):
        return pltpu.make_async_remote_copy(
            src_ref=ag_out,
            dst_ref=ag_in.at[i],
            send_sem=ag_send.at[0],
            recv_sem=ag_recv.at[i],
            device_id=(d, (m + i) % mp),
            device_id_type=MESH,
        )


    pl.semaphore_wait(barrier, n - 1 + mp - 1)

    for j in range(heads):
        cols = pl.ds(j * width, width)
        head = obuf[pl.ds(j, slots, stride=heads), :].astype(BF)
        att[:, cols] = head
        sent = nn_dot(disp[...], head)
        rows_out[:, :, cols] = sent.reshape(n, cap, width).astype(BF)
    rows_ex.start()
    rows_in[d] = rows_out[d]

    def block_product(i):
        w_copy(i).wait()
        part[i] = nn_dot(att[...], wbuf[i])

    messages = chain_messages(half)
    where = {message: i for i, message in enumerate(messages)}

    def slot_of(direction, left):
        return offsets.index(left if direction == 0 or left in (0, half) else -left)

    def lane_rows_of(direction, lane):
        upper = lane if direction == 0 else 1 - lane
        return pl.ds(upper * side, side)

    def msg_copy(direction, i):
        peer = (m + (1 if direction == 0 else mp - 1)) % mp
        return pltpu.make_async_remote_copy(
            src_ref=msg_out.at[direction, i],
            dst_ref=msg_in.at[direction, i],
            send_sem=msg_send.at[0],
            recv_sem=msg_recv.at[direction, i],
            device_id=(d, peer),
            device_id_type=MESH,
        )

    def send_message(i):
        left, lane = messages[i]
        for direction in range(2):
            rows = lane_rows_of(direction, lane)
            value = part[slot_of(direction, left), rows, :]
            came = where.get((left + 1, lane))
            if came is not None:
                msg_copy(direction, came).wait_recv()
                value = value + msg_in[direction, came].astype(F32)
            msg_out[direction, i] = value.astype(BF)
            msg_copy(direction, i).start()

    def finish_base():
        for lane in range(2):
            last = where[(1, lane)] if (1, lane) in where else None
            if last is None:
                continue
            for direction in range(2):
                rows = lane_rows_of(direction, lane)
                msg_copy(direction, last).wait_recv()
                base[rows, :] += msg_in[direction, last].astype(F32)

    def share_rows():
        rows_ex.arrived()
        got = rows_in[:, :, :features].astype(F32).reshape(codes, features).astype(BF)
        partial_low = nt_dot(got, shr[...])
        which = rows_in[:, :, features:].astype(F32).reshape(codes, 128)
        row = lax.broadcasted_iota(jnp.int32, (codes, 128), 0)
        second = ((row // half_group) % 2).astype(F32)
        placed = jnp.where(which == second, partial_low, pltpu.roll(partial_low, 64, 1))
        lane = lax.broadcasted_iota(jnp.int32, (half_group, 128), 1)
        for g in range(mp):
            r = g * group
            rs_out[g] = jnp.where(
                lane < 64,
                placed[r : r + half_group],
                placed[r + half_group : r + group],
            )
        rs_ex.start()
        rs_in[m] = rs_out[m]

    def sum_low():
        rs_ex.arrived()
        ag_out[...] = jnp.sum(rs_in[...], axis=0).astype(BF)
        for i in far_first_mp:
            low_copy(i).start()
        ag_in[0] = ag_out[...]

    sources = group // cap
    row = lax.broadcasted_iota(jnp.int32, (group, 128), 0)
    second_half = (row // half_group).astype(F32)
    lane_half = (lax.broadcasted_iota(jnp.int32, (group, 128), 1) // 64).astype(F32)

    def expand_group(i):
        if i:
            low_copy(i).wait_recv()
        first_source = ((m + mp - i) % mp) * sources
        low = ag_in[i].astype(F32)
        twice = jnp.concatenate([low, low], axis=0)
        which = (
            rows_in[pl.ds(first_source, sources), :, features:]
            .astype(F32)
            .reshape(group, 128)
        )
        moved = jnp.where(which == second_half, twice, pltpu.roll(twice, 64, 1))
        kept = jnp.where(which == lane_half, moved, 0.0).astype(BF)
        delta = 0.5 * nn_dot(kept, expw[...])
        back_out[pl.ds(first_source, sources)] = delta.reshape(
            sources, cap, outw
        ).astype(BF)
        for k in range(sources):
            source = first_source + k

            @pl.when(source != d)
            def _():
                pltpu.make_async_remote_copy(
                    src_ref=back_out.at[source],
                    dst_ref=back_in.at[d],
                    send_sem=back_sems.at[0],
                    recv_sem=back_sems.at[1],
                    device_id=(source, m),
                    device_id_type=MESH,
                ).start()

    def expand_low():
        for i in sorted(range(mp), key=lambda i: min(i, mp - i)):
            expand_group(i)
        back_in[d] = back_out[d]

    block_product(0)
    send_message(0)
    block_product(1)
    block_product(2)
    send_message(1)
    for i in range(3, mp - 1):
        block_product(i)
    w_copy(mp - 1).wait()
    base[...] = nn_dot(att[...], wbuf[mp - 1])
    send_message(2)
    send_message(3)
    share_rows()
    send_message(4)
    send_message(5)
    sum_low()
    send_message(6)
    expand_low()
    finish_base()

    back_ex.arrived()
    returned = back_in[...].astype(F32).reshape(codes, outw).astype(BF)
    correction = nn_dot(comb[...], returned)
    out_ref[...] = (live * (base[...] + correction)).astype(BF)

    for exchange in (rows_ex, back_ex, rs_ex):
        exchange.left()
    low_sent = ag_in.at[pl.ds(0, mp - 1)]
    pltpu.make_async_remote_copy(
        src_ref=low_sent,
        dst_ref=low_sent,
        send_sem=ag_send.at[0],
        recv_sem=ag_recv.at[1],
        device_id=(d, (m + 1) % mp),
        device_id_type=MESH,
    ).wait_send()
    pltpu.make_async_remote_copy(
        src_ref=msg_out,
        dst_ref=msg_in,
        send_sem=msg_send.at[0],
        recv_sem=msg_recv.at[0, 0],
        device_id=(d, (m + 1) % mp),
        device_id_type=MESH,
    ).wait_send()


def solution(mesh):
    n = mesh.shape["dp"]
    mp = mesh.shape["mp"]

    def body(
        queries,
        key_cache,
        value_cache,
        key_new,
        value_new,
        lengths,
        occupied,
        slot_request,
        request_adapter,
        out_weight,
        shrink_weight,
        expand_weight,
    ):
        slots, heads, width = queries.shape
        cached = key_cache.shape[2]
        features = heads * width
        outw = expand_weight.shape[2]
        cap = 2 * slots // n
        codes = n * cap
        ranks = shrink_weight.shape[0] * shrink_weight.shape[2]
        requests = request_adapter.shape[0]
        chunk = slots
        chunks = slots // chunk
        fetch = slots // 8
        fetches = slots // fetch
        messages = 2 * (mp // 2) - 1
        packed = codes // mp // 2
        any_spec = pl.BlockSpec(memory_space=pltpu.HBM)
        dma = pltpu.SemaphoreType.DMA
        return pl.pallas_call(
            functools.partial(kernel, n, mp, cap),
            out_shape=pltpu.VMEM((slots, outw), BF),
            in_specs=[any_spec] * 12,
            out_specs=pl.BlockSpec(memory_space=pltpu.VMEM),
            scratch_shapes=[
                pltpu.VMEM((1, slots), jnp.int32),
                pltpu.VMEM((1, slots), jnp.int32),
                pltpu.VMEM((1, slots), jnp.int32),
                pltpu.VMEM((requests // 128, 128), jnp.int32),
                pltpu.VMEM((slots * heads, width), BF),
                pltpu.VMEM((slots, cached, width), BF),
                pltpu.VMEM((slots, cached, width), BF),
                pltpu.VMEM((slots, width), BF),
                pltpu.VMEM((slots, width), BF),
                pltpu.VMEM((chunks, chunk * heads), F32),
                pltpu.VMEM((mp, features, outw), BF),
                pltpu.VMEM((ranks, features), BF),
                pltpu.VMEM((ranks, outw), BF),
                pltpu.VMEM((slots * heads, width), F32),
                pltpu.VMEM((slots, features), BF),
                pltpu.VMEM((codes, slots), BF),
                pltpu.VMEM((slots, codes), BF),
                pltpu.VMEM((n, cap, features + 128), BF),
                pltpu.VMEM((n, cap, features + 128), BF),
                pltpu.VMEM((mp, slots, outw), F32),
                pltpu.VMEM((2, messages, slots // 2, outw), BF),
                pltpu.VMEM((2, messages, slots // 2, outw), BF),
                pltpu.VMEM((slots, outw), F32),
                pltpu.VMEM((mp, packed, 128), F32),
                pltpu.VMEM((mp, packed, 128), F32),
                pltpu.VMEM((packed, 128), BF),
                pltpu.VMEM((mp, packed, 128), BF),
                pltpu.VMEM((n, cap, outw), BF),
                pltpu.VMEM((n, cap, outw), BF),
                dma((9,)),
                dma((fetches,)),
                dma((fetches,)),
                dma((mp,)),
                dma((2,)),
                dma((2,)),
                dma((1,)),
                dma((mp,)),
                dma((2,)),
                dma((1,)),
                dma((2, messages)),
            ],
            compiler_params=pltpu.CompilerParams(
                collective_id=0,
                has_side_effects=True,
                vmem_limit_bytes=60 << 20,
            ),
        )(
            lengths.reshape(1, slots),
            occupied.reshape(1, slots),
            slot_request.reshape(1, slots),
            request_adapter.reshape(requests // 128, 128),
            queries.reshape(slots * heads, width),
            key_cache.reshape(slots, cached, width),
            value_cache.reshape(slots, cached, width),
            key_new.reshape(slots, width),
            value_new.reshape(slots, width),
            out_weight,
            shrink_weight.transpose(0, 2, 1).reshape(ranks, features),
            expand_weight.reshape(ranks, outw),
        )

    placed = (
        P("dp", "mp", None),
        P("dp", "mp", None, None),
        P("dp", "mp", None, None),
        P("dp", "mp", None),
        P("dp", "mp", None),
        P("dp"),
        P("dp"),
        P("dp"),
        P(),
        P("mp", None),
        P("dp", "mp", None),
        P("dp", None, "mp"),
    )
    return jax.shard_map(
        body, mesh=mesh, in_specs=placed, out_specs=P("dp", "mp"), check_vma=False
    )
```

```python
import functools
import math

import jax
import jax.numpy as jnp
from jax import lax
from jax.experimental import pallas as pl
from jax.experimental.pallas import tpu as pltpu
from jax.sharding import PartitionSpec as P

MESH = pl.DeviceIdType.MESH
BF = jnp.bfloat16
F32 = jnp.float32


def nt_dot(a, b):
    return lax.dot_general(a, b, (((1,), (1,)), ((), ())), preferred_element_type=F32)


def nn_dot(a, b):
    return jnp.dot(a, b, preferred_element_type=F32)


def chain_messages(half):
    messages = [(half, 0)]
    for left in range(half - 1, 0, -1):
        messages += [(left, 1), (left, 0)]
    return messages


def kernel(
    n,
    mp,
    cap,
    lens_hbm,
    occ_hbm,
    sreq_hbm,
    radp_hbm,
    q_hbm,
    k_hbm,
    v_hbm,
    kn_hbm,
    vn_hbm,
    w_hbm,
    shr_hbm,
    exp_hbm,
    out_ref,
    lens,
    occ,
    sreq,
    radp,
    qbuf,
    kbuf,
    vbuf,
    knb,
    vnb,
    lens_wide,
    wbuf,
    shr,
    expw,
    obuf,
    att,
    disp,
    comb,
    rows_out,
    rows_in,
    part,
    msg_out,
    msg_in,
    base,
    rs_out,
    rs_in,
    ag_out,
    ag_in,
    back_out,
    back_in,
    small_sem,
    k_sem,
    v_sem,
    w_sem,
    rows_sems,
    rs_sems,
    ag_send,
    ag_recv,
    back_sems,
    msg_send,
    msg_recv,
):
    d = lax.axis_index("dp")
    m = lax.axis_index("mp")
    slots = lens.shape[1]
    heads = qbuf.shape[0] // slots
    width = qbuf.shape[1]
    outw = expw.shape[1]
    features = heads * width
    codes = n * cap
    group = codes // mp
    half_group = group // 2
    half = mp // 2
    inverse = 1.0 / math.sqrt(width)
    chunk = slots
    chunks = slots // chunk
    fetch = slots // 8
    fetches = slots // fetch
    side = slots // 2

    smalls = [
        pltpu.make_async_copy(src, dst, small_sem.at[i])
        for i, (src, dst) in enumerate(
            [
                (lens_hbm, lens),
                (q_hbm, qbuf),
                (kn_hbm, knb),
                (vn_hbm, vnb),
                (sreq_hbm, sreq),
                (radp_hbm, radp),
                (occ_hbm, occ),
                (shr_hbm, shr),
                (exp_hbm, expw),
            ]
        )
    ]

    def k_copy(c):
        rows = pl.ds(c * fetch, fetch)
        return pltpu.make_async_copy(k_hbm.at[rows], kbuf.at[rows], k_sem.at[c])

    def v_copy(c):
        rows = pl.ds(c * fetch, fetch)
        return pltpu.make_async_copy(v_hbm.at[rows], vbuf.at[rows], v_sem.at[c])

    offsets = [half]
    for r in range(half - 1, 0, -1):
        offsets += [r, -r]
    offsets += [0]

    def w_copy(i):
        block = (m + offsets[i] + mp) % mp
        cols = pl.ds(pl.multiple_of(block * outw, outw), outw)
        return pltpu.make_async_copy(w_hbm.at[:, cols], wbuf.at[i], w_sem.at[i])

    for copy in smalls[:4]:
        copy.start()
    for c in range(fetches):
        k_copy(c).start()
    for copy in smalls[4:]:
        copy.start()
    for c in range(fetches):
        v_copy(c).start()

    barrier = pltpu.get_barrier_semaphore()

    def greet_dp(i, carry):
        pl.semaphore_signal(
            barrier, inc=1, device_id=((d + i) % n, m), device_id_type=MESH
        )
        return carry

    def greet_mp(i, carry):
        pl.semaphore_signal(
            barrier, inc=1, device_id=(d, (m + i) % mp), device_id_type=MESH
        )
        return carry

    lax.fori_loop(1, n, greet_dp, 0)
    lax.fori_loop(1, mp, greet_mp, 0)

    for copy in smalls:
        copy.wait()

    request = sreq[...]
    high = request // 128
    low_part = request - high * 128
    lane_rows = lax.broadcasted_iota(jnp.int32, (128, slots), 0)
    hot_low = (lane_rows == low_part).astype(F32).astype(BF)
    table = nn_dot(radp[...].astype(F32).astype(BF), hot_low)
    high_rows = lax.broadcasted_iota(jnp.int32, table.shape, 0)
    adapter = jnp.sum(
        jnp.where(high_rows == high, table, 0.0), axis=0, keepdims=True
    ).astype(jnp.int32)
    owner = adapter // 2
    local_id = adapter - owner * 2
    owner_rows = lax.broadcasted_iota(jnp.int32, (n, slots), 0)
    hot_owner = (owner_rows == owner).astype(F32)
    before = (
        lax.broadcasted_iota(jnp.int32, (slots, slots), 0)
        < lax.broadcasted_iota(jnp.int32, (slots, slots), 1)
    ).astype(F32)
    earlier = nn_dot(hot_owner.astype(BF), before.astype(BF))
    position = jnp.sum(hot_owner * earlier, axis=0, keepdims=True).astype(jnp.int32)
    code = owner * cap + position
    code_rows = lax.broadcasted_iota(jnp.int32, (codes, slots), 0)
    hot_code = (code_rows == code).astype(F32)
    disp[...] = hot_code.astype(BF)
    ids = nn_dot(
        (hot_code * local_id.astype(F32)).astype(BF), jnp.ones((slots, 128), BF)
    )
    rows_out[:, :, features:] = ids.reshape(n, cap, 128).astype(BF)
    same = lax.broadcasted_iota(
        jnp.int32, (slots, slots), 0
    ) == lax.broadcasted_iota(jnp.int32, (slots, slots), 1)
    code_column = jnp.sum(
        jnp.where(same, code.astype(F32), 0.0), axis=1, keepdims=True
    ).astype(jnp.int32)
    comb[...] = (
        (lax.broadcasted_iota(jnp.int32, (slots, codes), 1) == code_column)
        .astype(F32)
        .astype(BF)
    )
    live = jnp.sum(
        jnp.where(same, occ[...].astype(F32), 0.0), axis=1, keepdims=True
    )

    span = chunk * heads
    lane_slot = lax.broadcasted_iota(jnp.int32, (chunk, span), 1) // heads
    row_slot = lax.broadcasted_iota(jnp.int32, (chunk, span), 0)
    own = (lane_slot == row_slot).astype(F32)
    positions = lax.broadcasted_iota(jnp.int32, (width, span), 0).astype(F32)
    slot_of_row = lax.broadcasted_iota(jnp.int32, (chunks, slots), 1)
    chunk_of_row = lax.broadcasted_iota(jnp.int32, (chunks, slots), 0)
    in_chunk = (slot_of_row // chunk == chunk_of_row).astype(F32)
    spread = (
        lax.broadcasted_iota(jnp.int32, (slots, span), 0) % chunk
        == lax.broadcasted_iota(jnp.int32, (slots, span), 1) // heads
    ).astype(F32)
    lens_wide[...] = nn_dot(
        (in_chunk * lens[...].astype(F32)).astype(BF), spread.astype(BF)
    )

    def attend(c, carry):
        rows = pl.ds(pl.multiple_of(c * span, span), span)
        first = c * chunk
        for f in range(chunk // fetch):
            k_copy(c * (chunk // fetch) + f).wait()
        tiles = []
        for p in range(chunk // 2):
            pair_rows = pl.ds(pl.multiple_of((first + 2 * p) * heads, 16), 2 * heads)
            keys = kbuf[pl.ds(first + 2 * p, 2)].reshape(2 * width, width)
            both = nt_dot(qbuf[pair_rows, :], keys)
            tiles += [both[:heads, :width], both[heads:, width:]]
        products = jnp.concatenate(tiles, axis=0).T * inverse
        new_keys = knb[pl.ds(pl.multiple_of(first, chunk), chunk), :]
        fresh = jnp.sum(
            own * nt_dot(new_keys, qbuf[rows, :]), axis=0, keepdims=True
        ) * inverse
        scores = jnp.where(
            positions < lens_wide[pl.ds(c, 1), :], products, -jnp.inf
        )
        top = jnp.maximum(jnp.max(scores, axis=0, keepdims=True), fresh)
        scores_exp = jnp.exp(scores - top)
        fresh_exp = jnp.exp(fresh - top)
        total = jnp.sum(scores_exp, axis=0, keepdims=True) + fresh_exp
        scale = 1.0 / total
        weights = (scores_exp * scale).T
        fresh_w = (own * (fresh_exp * scale)).astype(BF)
        new_values = vnb[pl.ds(pl.multiple_of(first, chunk), chunk), :]
        fresh_sum = lax.dot_general(
            fresh_w, new_values, (((0,), (0,)), ((), ())), preferred_element_type=F32
        )
        blank = jnp.zeros((heads, width), F32)
        for i in range(mp):
            w_copy(i).start()
        for f in range(chunk // fetch):
            v_copy(c * (chunk // fetch) + f).wait()
        sums = []
        for p in range(chunk // 2):
            r = 2 * p * heads
            pair = jnp.concatenate(
                [
                    jnp.concatenate([weights[r : r + heads], blank], axis=1),
                    jnp.concatenate([blank, weights[r + heads : r + 2 * heads]], axis=1),
                ],
                axis=0,
            ).astype(BF)
            values = vbuf[pl.ds(first + 2 * p, 2)].reshape(2 * width, width)
            sums.append(nn_dot(pair, values))
        obuf[rows, :] = jnp.concatenate(sums, axis=0) + fresh_sum
        return carry

    attend(0, 0)

    ring = math.isqrt(n // 2)

    def peer_of(i):
        dx, dy, dc = i // (2 * ring), (i // 2) % ring, i % 2
        x = (d // (2 * ring) + dx) % ring
        y = ((d // 2) % ring + dy) % ring
        return (x * ring + y) * 2 + (d + dc) % 2

    def hops(i):
        dx, dy = i // (2 * ring), (i // 2) % ring
        return min(dx, ring - dx) + min(dy, ring - dy)

    far_first_dp = sorted(range(1, n), key=lambda i: -hops(i))
    far_first_mp = sorted(range(1, mp), key=lambda i: -min(i, mp - i))

    class Exchange:
        def __init__(self, out, landing, sems, over_dp, same_for_all=False):
            self.count = n if over_dp else mp
            self.out, self.landing, self.sems = out, landing, sems
            self.over_dp, self.same_for_all = over_dp, same_for_all

        def device(self, i):
            if not self.over_dp:
                return (d, (m + i) % mp)
            return (peer_of(i), m)

        def start(self):
            here = d if self.over_dp else m
            for i in far_first_dp if self.over_dp else far_first_mp:
                device = self.device(i)
                peer = device[0] if self.over_dp else device[1]
                pltpu.make_async_remote_copy(
                    src_ref=self.out if self.same_for_all else self.out.at[peer],
                    dst_ref=self.landing.at[here],
                    send_sem=self.sems.at[0],
                    recv_sem=self.sems.at[1],
                    device_id=device,
                    device_id_type=MESH,
                ).start()

        def whole(self):
            all_blocks = self.landing.at[pl.ds(0, self.count - 1)]
            return pltpu.make_async_remote_copy(
                src_ref=all_blocks,
                dst_ref=all_blocks,
                send_sem=self.sems.at[0],
                recv_sem=self.sems.at[1],
                device_id=self.device(1),
                device_id_type=MESH,
            )

        def arrived(self):
            self.whole().wait_recv()

        def left(self):
            self.whole().wait_send()

    rows_ex = Exchange(rows_out, rows_in, rows_sems, True)
    back_ex = Exchange(back_out, back_in, back_sems, True)
    rs_ex = Exchange(rs_out, rs_in, rs_sems, False)

    def low_copy(i):
        return pltpu.make_async_remote_copy(
            src_ref=ag_out,
            dst_ref=ag_in.at[i],
            send_sem=ag_send.at[0],
            recv_sem=ag_recv.at[i],
            device_id=(d, (m + i) % mp),
            device_id_type=MESH,
        )


    pl.semaphore_wait(barrier, n - 1 + mp - 1)

    for j in range(heads):
        cols = pl.ds(j * width, width)
        head = obuf[pl.ds(j, slots, stride=heads), :].astype(BF)
        att[:, cols] = head
        sent = nn_dot(disp[...], head)
        rows_out[:, :, cols] = sent.reshape(n, cap, width).astype(BF)
    rows_ex.start()
    rows_in[d] = rows_out[d]

    def block_product(i):
        w_copy(i).wait()
        part[i] = nn_dot(att[...], wbuf[i])

    messages = chain_messages(half)
    where = {message: i for i, message in enumerate(messages)}

    def slot_of(direction, left):
        return offsets.index(left if direction == 0 or left in (0, half) else -left)

    def lane_rows_of(direction, lane):
        upper = lane if direction == 0 else 1 - lane
        return pl.ds(upper * side, side)

    def msg_copy(direction, i):
        peer = (m + (1 if direction == 0 else mp - 1)) % mp
        return pltpu.make_async_remote_copy(
            src_ref=msg_out.at[direction, i],
            dst_ref=msg_in.at[direction, i],
            send_sem=msg_send.at[0],
            recv_sem=msg_recv.at[direction, i],
            device_id=(d, peer),
            device_id_type=MESH,
        )

    def send_message(i):
        left, lane = messages[i]
        for direction in range(2):
            rows = lane_rows_of(direction, lane)
            value = part[slot_of(direction, left), rows, :]
            came = where.get((left + 1, lane))
            if came is not None:
                msg_copy(direction, came).wait_recv()
                value = value + msg_in[direction, came].astype(F32)
            msg_out[direction, i] = value.astype(BF)
            msg_copy(direction, i).start()

    def finish_base():
        for lane in range(2):
            last = where[(1, lane)] if (1, lane) in where else None
            if last is None:
                continue
            for direction in range(2):
                rows = lane_rows_of(direction, lane)
                msg_copy(direction, last).wait_recv()
                base[rows, :] += msg_in[direction, last].astype(F32)

    def share_rows():
        rows_ex.arrived()
        got = rows_in[:, :, :features].astype(F32).reshape(codes, features).astype(BF)
        partial_low = nt_dot(got, shr[...])
        which = rows_in[:, :, features:].astype(F32).reshape(codes, 128)
        row = lax.broadcasted_iota(jnp.int32, (codes, 128), 0)
        second = ((row // half_group) % 2).astype(F32)
        placed = jnp.where(which == second, partial_low, pltpu.roll(partial_low, 64, 1))
        lane = lax.broadcasted_iota(jnp.int32, (half_group, 128), 1)
        for g in range(mp):
            r = g * group
            rs_out[g] = jnp.where(
                lane < 64,
                placed[r : r + half_group],
                placed[r + half_group : r + group],
            ).astype(BF)
        rs_ex.start()
        rs_in[m] = rs_out[m]

    def sum_low():
        rs_ex.arrived()
        ag_out[...] = jnp.sum(rs_in[...].astype(F32), axis=0).astype(BF)
        for i in far_first_mp:
            low_copy(i).start()
        ag_in[0] = ag_out[...]

    sources = group // cap
    row = lax.broadcasted_iota(jnp.int32, (group, 128), 0)
    second_half = (row // half_group).astype(F32)
    lane_half = (lax.broadcasted_iota(jnp.int32, (group, 128), 1) // 64).astype(F32)

    def expand_group(i):
        if i:
            low_copy(i).wait_recv()
        first_source = ((m + mp - i) % mp) * sources
        low = ag_in[i].astype(F32)
        twice = jnp.concatenate([low, low], axis=0)
        which = (
            rows_in[pl.ds(first_source, sources), :, features:]
            .astype(F32)
            .reshape(group, 128)
        )
        moved = jnp.where(which == second_half, twice, pltpu.roll(twice, 64, 1))
        kept = jnp.where(which == lane_half, moved, 0.0).astype(BF)
        delta = 0.5 * nn_dot(kept, expw[...])
        back_out[pl.ds(first_source, sources)] = delta.reshape(
            sources, cap, outw
        ).astype(BF)
        for k in range(sources):
            source = first_source + k

            @pl.when(source != d)
            def _():
                pltpu.make_async_remote_copy(
                    src_ref=back_out.at[source],
                    dst_ref=back_in.at[d],
                    send_sem=back_sems.at[0],
                    recv_sem=back_sems.at[1],
                    device_id=(source, m),
                    device_id_type=MESH,
                ).start()

    def expand_low():
        for i in sorted(range(mp), key=lambda i: min(i, mp - i)):
            expand_group(i)
        back_in[d] = back_out[d]

    block_product(0)
    send_message(0)
    block_product(1)
    block_product(2)
    send_message(1)
    for i in range(3, mp - 1):
        block_product(i)
    w_copy(mp - 1).wait()
    base[...] = nn_dot(att[...], wbuf[mp - 1])
    send_message(2)
    send_message(3)
    share_rows()
    send_message(4)
    send_message(5)
    sum_low()
    send_message(6)
    expand_low()
    finish_base()

    back_ex.arrived()
    returned = back_in[...].astype(F32).reshape(codes, outw).astype(BF)
    correction = nn_dot(comb[...], returned)
    out_ref[...] = (live * (base[...] + correction)).astype(BF)

    for exchange in (rows_ex, back_ex, rs_ex):
        exchange.left()
    low_sent = ag_in.at[pl.ds(0, mp - 1)]
    pltpu.make_async_remote_copy(
        src_ref=low_sent,
        dst_ref=low_sent,
        send_sem=ag_send.at[0],
        recv_sem=ag_recv.at[1],
        device_id=(d, (m + 1) % mp),
        device_id_type=MESH,
    ).wait_send()
    pltpu.make_async_remote_copy(
        src_ref=msg_out,
        dst_ref=msg_in,
        send_sem=msg_send.at[0],
        recv_sem=msg_recv.at[0, 0],
        device_id=(d, (m + 1) % mp),
        device_id_type=MESH,
    ).wait_send()


def solution(mesh):
    n = mesh.shape["dp"]
    mp = mesh.shape["mp"]

    def body(
        queries,
        key_cache,
        value_cache,
        key_new,
        value_new,
        lengths,
        occupied,
        slot_request,
        request_adapter,
        out_weight,
        shrink_weight,
        expand_weight,
    ):
        slots, heads, width = queries.shape
        cached = key_cache.shape[2]
        features = heads * width
        outw = expand_weight.shape[2]
        cap = 2 * slots // n
        codes = n * cap
        ranks = shrink_weight.shape[0] * shrink_weight.shape[2]
        requests = request_adapter.shape[0]
        chunk = slots
        chunks = slots // chunk
        fetch = slots // 8
        fetches = slots // fetch
        messages = 2 * (mp // 2) - 1
        packed = codes // mp // 2
        any_spec = pl.BlockSpec(memory_space=pltpu.HBM)
        dma = pltpu.SemaphoreType.DMA
        return pl.pallas_call(
            functools.partial(kernel, n, mp, cap),
            out_shape=pltpu.VMEM((slots, outw), BF),
            in_specs=[any_spec] * 12,
            out_specs=pl.BlockSpec(memory_space=pltpu.VMEM),
            scratch_shapes=[
                pltpu.VMEM((1, slots), jnp.int32),
                pltpu.VMEM((1, slots), jnp.int32),
                pltpu.VMEM((1, slots), jnp.int32),
                pltpu.VMEM((requests // 128, 128), jnp.int32),
                pltpu.VMEM((slots * heads, width), BF),
                pltpu.VMEM((slots, cached, width), BF),
                pltpu.VMEM((slots, cached, width), BF),
                pltpu.VMEM((slots, width), BF),
                pltpu.VMEM((slots, width), BF),
                pltpu.VMEM((chunks, chunk * heads), F32),
                pltpu.VMEM((mp, features, outw), BF),
                pltpu.VMEM((ranks, features), BF),
                pltpu.VMEM((ranks, outw), BF),
                pltpu.VMEM((slots * heads, width), F32),
                pltpu.VMEM((slots, features), BF),
                pltpu.VMEM((codes, slots), BF),
                pltpu.VMEM((slots, codes), BF),
                pltpu.VMEM((n, cap, features + 128), BF),
                pltpu.VMEM((n, cap, features + 128), BF),
                pltpu.VMEM((mp, slots, outw), F32),
                pltpu.VMEM((2, messages, slots // 2, outw), BF),
                pltpu.VMEM((2, messages, slots // 2, outw), BF),
                pltpu.VMEM((slots, outw), F32),
                pltpu.VMEM((mp, packed, 128), BF),
                pltpu.VMEM((mp, packed, 128), BF),
                pltpu.VMEM((packed, 128), BF),
                pltpu.VMEM((mp, packed, 128), BF),
                pltpu.VMEM((n, cap, outw), BF),
                pltpu.VMEM((n, cap, outw), BF),
                dma((9,)),
                dma((fetches,)),
                dma((fetches,)),
                dma((mp,)),
                dma((2,)),
                dma((2,)),
                dma((1,)),
                dma((mp,)),
                dma((2,)),
                dma((1,)),
                dma((2, messages)),
            ],
            compiler_params=pltpu.CompilerParams(
                collective_id=0,
                has_side_effects=True,
                vmem_limit_bytes=60 << 20,
            ),
        )(
            lengths.reshape(1, slots),
            occupied.reshape(1, slots),
            slot_request.reshape(1, slots),
            request_adapter.reshape(requests // 128, 128),
            queries.reshape(slots * heads, width),
            key_cache.reshape(slots, cached, width),
            value_cache.reshape(slots, cached, width),
            key_new.reshape(slots, width),
            value_new.reshape(slots, width),
            out_weight,
            shrink_weight.transpose(0, 2, 1).reshape(ranks, features),
            expand_weight.reshape(ranks, outw),
        )

    placed = (
        P("dp", "mp", None),
        P("dp", "mp", None, None),
        P("dp", "mp", None, None),
        P("dp", "mp", None),
        P("dp", "mp", None),
        P("dp"),
        P("dp"),
        P("dp"),
        P(),
        P("mp", None),
        P("dp", "mp", None),
        P("dp", None, "mp"),
    )
    return jax.shard_map(
        body, mesh=mesh, in_specs=placed, out_specs=P("dp", "mp"), check_vma=False
    )
```
